256 devices in a mesh: dp: 8 (over y, core), expert: 32 (over z, x).
Axes of the slice: x: 4, y: 4, z: 8, core: 2. Of those that a mesh axis runs over, the one named last changes fastest.
Arguments:
- tokens: bfloat16 [32768, 2560], P(('dp', 'expert')), may hold values from -6 to 6
- cotangent: bfloat16 [32768, 2560], P(('dp', 'expert')), may hold values from -6 to 6
- routes: int32 [32768, 1], P(('dp', 'expert')), may hold values from 0 to 31; in each aligned block of 128 rows (0 to 127, 128 to 255, ...) at most 6 rows name the same one
- gates: float32 [32768, 1], P(('dp', 'expert')), may hold values from 0.25 to 1
- hot_index: int32 [4096], P(('dp', 'expert')), may hold values from 0 to 127, as said below
- hot_gate: float32 [4096], P(('dp', 'expert')), may hold values from 0.25 to 1
- w_gate_up: bfloat16 [32, 2560, 1536], P('expert', 'dp'), may hold values from -0.125 to 0.125
- w_down: bfloat16 [32, 768, 2560], P('expert', 'dp'), may hold values from -0.21875 to 0.21875
- w_hot_gu: bfloat16 [2, 768, 2560], P(None, 'dp', 'expert'), may hold values from -0.125 to 0.125
- w_hot_dn: bfloat16 [768, 2560], P('dp', 'expert'), may hold values from -0.21875 to 0.21875
Outputs:
- layer_out: bfloat16 [32768, 2560], P(('dp', 'expert'))
- input_grad: bfloat16 [32768, 2560], P(('dp', 'expert'))
- grad_gate_up: bfloat16 [32, 2560, 1536], P('expert', 'dp')
- grad_down: bfloat16 [32, 768, 2560], P('expert', 'dp')
- grad_hot_gu: bfloat16 [2, 768, 2560], P(None, 'dp', 'expert')
- grad_hot_dn: bfloat16 [768, 2560], P('dp', 'expert')
The draws below stay inside these ranges and needn't reach their ends.
Inputs may be any that keep to these rules, and one draw needn't show every extreme that they name: `routes`: each token names 1 different routed experts; the tokens of one device name any one routed expert at most 6 times, some expert exactly 6 times. `hot_index`: the 16 entries of one device name different tokens of that device, by their index within the device.
All inputs are finite; a program needn't handle non-finite values.
Results may differ from the reference program's by a relative error of at most 0.018.
Values may be sent and summed in bfloat16 or wider, within the bound.
A program may use at most 128 MiB of HBM per device.

```python
import math
import jax
import jax.numpy as jnp
import numpy as np
from jax import lax

D = 2560
H = 768
TOPK = 1
TOK_DEV = 128
HOT_DEV = 16
EXPERTS = 32
CAP = 6
GRAD_DIV = 32
TOKENS = 32768
TOKENS_HOT = 4096
N_DP = 8
N_EXPERT = 32


def draw_hot_index(key, part):
    blocks = TOKENS // TOK_DEV
    keys = jax.random.split(key, blocks)
    picks = jax.vmap(lambda one: jax.random.permutation(one, TOK_DEV)[:HOT_DEV])(keys)
    return picks.reshape(-1).astype(jnp.int32)


def block_scale(stream_key, extent, cuts, low, top_value):
    def one(dim, blocks):
        heights = jax.random.uniform(jax.random.fold_in(jax.random.fold_in(stream_key, 6), dim), (blocks,), jnp.float32, low / len(cuts), top_value / len(cuts))
        return jnp.repeat(jnp.exp(heights), extent[dim] // blocks).reshape((-1,) + (1,) * (len(extent) - dim - 1))

    gain = one(*cuts[0])
    for cut in cuts[1:]:
        gain = gain * one(*cut)
    return gain


def assign_block(stream_key, own, number, rows, amount, top, reach, slope):
    sequence = jax.random.permutation(stream_key, amount)
    packed, common = portions_of(amount, rows * top, reach, slope, True), portions_of(amount, rows * top, reach, slope, False)
    places = jnp.arange(amount)

    def named(lengths, rotation):
        used = int((lengths > 0).sum())
        fixed = max(1, used // 4)
        passed = fixed + (places - fixed + rotation * (used - fixed)) % max(1, amount - fixed)
        return jnp.zeros((amount,), jnp.int32).at[sequence[jnp.where(places < fixed, places, passed)]].set(jnp.asarray(lengths, jnp.int32))

    lengths = jnp.where(number % 4 == 0, named(packed, number // 4), named(common, number - number // 4 - 1))
    mixed = jax.random.permutation(jax.random.fold_in(own, 3), amount)
    giver, sink = mixed[0:amount // 2 * 2:2], mixed[1:amount // 2 * 2:2]
    room = jnp.minimum(lengths[giver] - 1, reach - lengths[sink]) // 2
    room = jnp.where((giver == sequence[0]) | (sink == sequence[0]) | (lengths[sink] == 0), 0, jnp.maximum(room, 0))
    passed = jax.random.randint(jax.random.fold_in(own, 4), (amount // 2,), 0, 1 << 20) % (room + 1)
    lengths = lengths.at[giver].add(-passed).at[sink].add(passed)
    items = jnp.searchsorted(jnp.cumsum(lengths), jnp.arange(rows * top), side="right").astype(jnp.int32)
    table = items.reshape(top, rows).T
    table = table[jax.random.permutation(jax.random.fold_in(own, 1), rows)]
    rotation = jax.random.randint(jax.random.fold_in(own, 2), (rows, 1), 0, top)
    return jnp.take_along_axis(table, (jnp.arange(top)[None, :] + rotation) % top, axis=1)


def portions_of(count, total, limit, slope, full):
    portions = [(1 << 20) // math.isqrt(standing ** slope) + 1 for standing in range(1, count + 1)]
    largest = limit if full else min(limit, max(-(-total // count), total * portions[0] // sum(portions)))
    least = 1 if total - largest >= count - 1 else 0
    counts, surplus = [largest] + [least] * (count - 1), total - largest - least * (count - 1)
    while surplus > 0:
        movable = [i for i in range(1, count) if counts[i] < largest] or [i for i in range(1, count) if counts[i] < limit]
        pool, budget = sum([portions[i] for i in movable]), surplus
        for i in movable:
            more = min(limit - counts[i], max(1, budget * portions[i] // pool), surplus)
            counts[i] = counts[i] + more
            surplus = surplus - more
    return np.array(counts)


def centred(key, extent, scale, reach, cuts=(), kind=jnp.bfloat16):
    values = scale * jax.random.normal(key, extent, jnp.float32)
    if cuts:
        values = values * block_scale(key, extent, cuts, -0.22, 0.18)
    return jnp.clip(values, -reach, reach).astype(kind)


def setup_inputs(seed: int = 0) -> dict:
    key_of = jax.random.split(jax.random.key(seed), 11)
    tokens = centred(key_of[0], (TOKENS, D), 1.0, 6.0, ((0, 256),))
    cotangent = centred(key_of[1], (TOKENS, D), 1.0, 6.0, ((0, 256),))
    routes_keys = jax.random.split(jax.random.fold_in(key_of[2], 1), TOKENS // TOK_DEV)
    routes_turns = jax.random.permutation(jax.random.fold_in(key_of[2], 3), TOKENS // TOK_DEV)
    routes = jax.vmap(lambda own, number: assign_block(jax.random.fold_in(key_of[2], 2), own, number, TOK_DEV, EXPERTS, TOPK, CAP, 2))(routes_keys, routes_turns).reshape((TOKENS, TOPK))
    gates = jnp.clip(0.25 + 0.75 * jax.random.uniform(key_of[3], (TOKENS, TOPK), jnp.float32) ** block_scale(key_of[3], (TOKENS, TOPK), ((0, 256),), -0.2, 0.2), 0.25, 1.0)
    hot_index = draw_hot_index(jax.random.fold_in(key_of[10], 71), 0)
    hot_gate = jnp.clip(0.25 + 0.75 * jax.random.uniform(key_of[5], (TOKENS_HOT,), jnp.float32) ** block_scale(key_of[5], (TOKENS_HOT,), ((0, 256),), -0.2, 0.2), 0.25, 1.0)
    w_gate_up = centred(key_of[6], (EXPERTS, D, 2 * H), D ** -0.5, 0.125, ((0, 32), (1, 8)))
    w_down = centred(key_of[7], (EXPERTS, H, D), H ** -0.5, 0.21875, ((0, 32), (1, 8)))
    w_hot_gu = centred(key_of[8], (2, H, D), D ** -0.5, 0.125, ((1, 8), (2, 32)))
    w_hot_dn = centred(key_of[9], (H, D), H ** -0.5, 0.21875, ((0, 8), (1, 32)))
    return {"tokens": tokens, "cotangent": cotangent, "routes": routes, "gates": gates, "hot_index": hot_index, "hot_gate": hot_gate, "w_gate_up": w_gate_up, "w_down": w_down, "w_hot_gu": w_hot_gu, "w_hot_dn": w_hot_dn}


def slot_positions(route_block, count):
    flat = route_block.reshape(-1).astype(jnp.int32)
    onehot = (flat[:, None] == jnp.arange(count, dtype=jnp.int32)[None, :]).astype(jnp.int32)
    before = jnp.cumsum(onehot, axis=0) - onehot
    return flat, jnp.sum(before * onehot, axis=1).astype(jnp.int32)


def expert_forward(rows_x, w_gu):
    width = w_gu.shape[1] // 2
    act = jnp.dot(rows_x, w_gu, preferred_element_type=jnp.float32)
    gate_part = act[:, :width]
    up_part = act[:, width:]
    hidden = (gate_part * jax.nn.sigmoid(gate_part) * up_part).astype(jnp.bfloat16)
    return act, hidden


def expert_output(hidden, w_dn):
    return jnp.dot(hidden, w_dn, preferred_element_type=jnp.float32).astype(jnp.bfloat16)


def expert_delta(scaled_rows, act, w_gu, w_dn):
    width = w_gu.shape[1] // 2
    gate_part = act[:, :width]
    up_part = act[:, width:]
    sigma = jax.nn.sigmoid(gate_part)
    d_hidden = lax.dot_general(scaled_rows, w_dn, (((1,), (1,)), ((), ())), preferred_element_type=jnp.float32)
    d_gate = d_hidden * up_part * sigma * (1.0 + gate_part * (1.0 - sigma))
    d_up = d_hidden * gate_part * sigma
    d_act = jnp.concatenate([d_gate, d_up], axis=1).astype(jnp.bfloat16)
    d_rows = lax.dot_general(d_act, w_gu, (((1,), (1,)), ((), ())), preferred_element_type=jnp.float32).astype(jnp.bfloat16)
    return d_act, d_rows


def popular_expert(tokens, cotangent, hot_index, hot_gate, w_hot_gu, w_hot_dn):
    blocks = N_DP * N_EXPERT
    local = hot_index.reshape(blocks, HOT_DEV).astype(jnp.int32)
    global_rows = (local + jnp.arange(blocks, dtype=jnp.int32)[:, None] * TOK_DEV).reshape(-1).astype(jnp.int32)
    hot_x = tokens[global_rows]
    hot_s = (hot_gate[:, None] * cotangent[global_rows].astype(jnp.float32)).astype(jnp.bfloat16)
    feature_dims = (((1,), (1,)), ((), ()))
    gate_part = lax.dot_general(hot_x, w_hot_gu[0], feature_dims, preferred_element_type=jnp.float32)
    up_part = lax.dot_general(hot_x, w_hot_gu[1], feature_dims, preferred_element_type=jnp.float32)
    sigma = jax.nn.sigmoid(gate_part)
    hidden = (gate_part * sigma * up_part).astype(jnp.bfloat16)
    hot_out = jnp.dot(hidden, w_hot_dn, preferred_element_type=jnp.float32)
    d_hidden = lax.dot_general(hot_s, w_hot_dn, feature_dims, preferred_element_type=jnp.float32)
    d_gate = (d_hidden * up_part * sigma * (1.0 + gate_part * (1.0 - sigma))).astype(jnp.bfloat16)
    d_up = (d_hidden * gate_part * sigma).astype(jnp.bfloat16)
    hot_back = jnp.dot(d_gate, w_hot_gu[0], preferred_element_type=jnp.float32) + jnp.dot(d_up, w_hot_gu[1], preferred_element_type=jnp.float32)
    inverse = 1.0 / GRAD_DIV

    def by_column(array):
        width = array.shape[-1]
        return array.reshape(N_DP, N_EXPERT, HOT_DEV, width).transpose(1, 0, 2, 3).reshape(N_EXPERT, N_DP * HOT_DEV, width)

    def column(carry, piece):
        acc_gu, acc_dn = carry
        col_x, col_g, col_u, col_h, col_s = piece
        row_dims = (((0,), (0,)), ((), ()))
        part_gu = jnp.stack([lax.dot_general(col_g, col_x, row_dims, preferred_element_type=jnp.float32), lax.dot_general(col_u, col_x, row_dims, preferred_element_type=jnp.float32)]) * inverse
        part_dn = lax.dot_general(col_h, col_s, row_dims, preferred_element_type=jnp.float32) * inverse
        acc_gu = acc_gu + lax.optimization_barrier(part_gu.astype(jnp.bfloat16)).astype(jnp.float32)
        acc_dn = acc_dn + lax.optimization_barrier(part_dn.astype(jnp.bfloat16)).astype(jnp.float32)
        return (acc_gu, acc_dn), None

    init = (jnp.zeros(w_hot_gu.shape, jnp.float32), jnp.zeros(w_hot_dn.shape, jnp.float32))
    (acc_gu, acc_dn), unused = lax.scan(column, init, (by_column(hot_x), by_column(d_gate), by_column(d_up), by_column(hidden), by_column(hot_s)))
    return global_rows, hot_out, hot_back, acc_gu.astype(jnp.bfloat16), acc_dn.astype(jnp.bfloat16)


def reference(tokens, cotangent, routes, gates, hot_index, hot_gate, w_gate_up, w_down, w_hot_gu, w_hot_dn):
    width_d = tokens.shape[1]
    inverse = 1.0 / GRAD_DIV
    entries = TOK_DEV * TOPK
    total = EXPERTS * N_EXPERT * CAP
    x_groups = tokens.reshape(N_DP, N_EXPERT, TOK_DEV, width_d)
    dy_groups = cotangent.reshape(N_DP, N_EXPERT, TOK_DEV, width_d)
    r_groups = routes.reshape(N_DP, N_EXPERT, TOK_DEV, TOPK)
    g_groups = gates.reshape(N_DP, N_EXPERT, TOK_DEV, TOPK)

    def one_group(carry, item):
        acc_gu, acc_dn = carry
        x_g, dy_g, r_g, g_g = item
        flat, pos = jax.vmap(lambda block: slot_positions(block, EXPERTS))(r_g)
        source = jnp.arange(N_EXPERT, dtype=jnp.int32)[:, None]
        entry = jnp.arange(entries, dtype=jnp.int32)[None, :]
        dest = (flat * (N_EXPERT * CAP) + source * CAP + pos).reshape(-1).astype(jnp.int32)
        entry_ids = (source * entries + entry).reshape(-1).astype(jnp.int32)
        table = jnp.full((total,), N_EXPERT * entries, jnp.int32).at[dest].set(entry_ids)
        gate_flat = g_g.reshape(N_EXPERT * entries)
        scaled = (g_g[:, :, :, None] * dy_g[:, :, None, :].astype(jnp.float32)).astype(jnp.bfloat16)
        scaled_pad = jnp.concatenate([scaled.reshape(-1, width_d), jnp.zeros((1, width_d), jnp.bfloat16)], axis=0)
        x_pad = jnp.concatenate([x_g.reshape(-1, width_d), jnp.zeros((1, width_d), jnp.bfloat16)], axis=0)
        rows_x = x_pad[table // TOPK].reshape(EXPERTS, N_EXPERT * CAP, width_d)
        rows_s = scaled_pad[table].reshape(EXPERTS, N_EXPERT * CAP, width_d)

        def per_expert(piece):
            rx, rs, wgu, wdn = piece
            act, hidden = expert_forward(rx, wgu)
            out = expert_output(hidden, wdn)
            d_act, d_rows = expert_delta(rs, act, wgu, wdn)
            grad_gu = lax.dot_general(rx, d_act, (((0,), (0,)), ((), ())), preferred_element_type=jnp.float32) * inverse
            grad_dn = lax.dot_general(hidden, rs, (((0,), (0,)), ((), ())), preferred_element_type=jnp.float32) * inverse
            return out, d_rows, grad_gu, grad_dn

        out, d_rows, grad_gu, grad_dn = lax.map(per_expert, (rows_x, rows_s, w_gate_up, w_down))
        acc_gu = acc_gu + lax.optimization_barrier(grad_gu.astype(jnp.bfloat16)).astype(jnp.float32)
        acc_dn = acc_dn + lax.optimization_barrier(grad_dn.astype(jnp.bfloat16)).astype(jnp.float32)
        picked = out.reshape(total, width_d)[dest].astype(jnp.float32)
        layer_out = (gate_flat[:, None] * picked).reshape(N_EXPERT, TOK_DEV, TOPK, width_d).sum(axis=2)
        back = d_rows.reshape(total, width_d)[dest].astype(jnp.float32)
        input_grad = back.reshape(N_EXPERT, TOK_DEV, TOPK, width_d).sum(axis=2)
        return (acc_gu, acc_dn), (layer_out, input_grad)

    init = (jnp.zeros(w_gate_up.shape, jnp.float32), jnp.zeros(w_down.shape, jnp.float32))
    (acc_gu, acc_dn), (outs, grads) = lax.scan(one_group, init, (x_groups, dy_groups, r_groups, g_groups))
    global_rows, hot_out, hot_back, hot_gu, hot_dn = popular_expert(tokens, cotangent, hot_index, hot_gate, w_hot_gu, w_hot_dn)
    layer_all = outs.reshape(TOKENS, width_d).at[global_rows].add(hot_gate[:, None] * hot_out)
    grad_all = grads.reshape(TOKENS, width_d).at[global_rows].add(hot_back)
    return (layer_all.astype(jnp.bfloat16), grad_all.astype(jnp.bfloat16), acc_gu.astype(jnp.bfloat16), acc_dn.astype(jnp.bfloat16), hot_gu, hot_dn)
```

```python
import functools

import jax
import jax.numpy as jnp
import numpy as np
from jax import lax
from jax.experimental import pallas as pl
from jax.experimental.pallas import tpu as pltpu
from jax.sharding import PartitionSpec as P

MESH = pl.DeviceIdType.MESH
BF = jnp.bfloat16
F32 = jnp.float32
CAP = 6
MSG = 16
NZ, NX, NY = 8, 4, 4


def dot(a, b):
    return jnp.dot(a, b, preferred_element_type=F32)


def dot_nt(a, b):
    return lax.dot_general(a, b, (((1,), (1,)), ((), ())), preferred_element_type=F32)


def hit(a, b):
    return jnp.where(a == b, 1.0, 0.0).astype(BF)


def iota(shape, axis):
    return lax.broadcasted_iota(jnp.int32, shape, axis)


class Sems:
    def __init__(self, send, recv):
        self.send, self.recv, self.ids = send, recv, {}

    def __call__(self, name):
        if name not in self.ids:
            self.ids[name] = len(self.ids)
        n = self.ids[name]
        return self.send.at[n], self.recv.at[n]


def kernel(
    tok, cot, routes_row, routes_col, gates, hidx_row, hidx_col, hgate, perm_col, perm_row,
    wgu_in, wdn_in, hw_in,
    lo_out, ig_out, ggu_out, gdn_out, ghw_out,
    wgu, wdn, hxs, hw, msend, mrecv, mback, rxs, xt, ht, hid, dact,
    pgu, pdn, phb, qgu, qdn, qhb, rgu, rdn, rhb, hown, hg, hgr, hgz,
    sem_s, sem_r, a_s, a_r, b_s, b_r, loc,
):
    me, e = lax.axis_index("dp"), lax.axis_index("expert")
    y, c = me // 2, me % 2
    z, x = e // NX, e % NX
    yp, ym, y2 = (y + 1) % NY, (y + 3) % NY, (y + 2) % NY
    xp, xm, x2 = (x + 1) % NX, (x + 3) % NX, (x + 2) % NX
    up, down, mate = (2 * yp + c, e), (2 * ym + c, e), (2 * y + 1 - c, e)
    right, left = (me, NX * z + xp), (me, NX * z + xm)
    sems = Sems(sem_s, sem_r)
    started = []

    def send(name, src, dst, dev):
        s, r = sems(name)
        copy = pltpu.make_async_remote_copy(
            src_ref=src, dst_ref=dst, send_sem=s, recv_sem=r, device_id=dev, device_id_type=MESH
        )
        copy.start()
        started.append(copy)

    def arrived(name, dst):
        s, r = sems(name)
        pltpu.make_async_remote_copy(
            src_ref=dst, dst_ref=dst, send_sem=s, recv_sem=r, device_id=mate, device_id_type=MESH
        ).wait_recv()

    barrier = pltpu.get_barrier_semaphore()
    for dev in (up, down, mate):
        pl.semaphore_signal(barrier, inc=1, device_id=dev, device_id_type=MESH)

    @pl.loop(1, NZ * NX)
    def _(j):
        pl.semaphore_signal(
            barrier, inc=1, device_id=(me, (e + j) % (NZ * NX)), device_id_type=MESH
        )

    own_gu = pltpu.make_async_copy(wgu_in.at[0], wgu.at[me], loc.at[0])
    own_dn = pltpu.make_async_copy(wdn_in.at[0], wdn.at[me], loc.at[1])
    own_gu.start()
    own_dn.start()

    n_tok, width = tok.shape
    third = 3 * width // 4 // 3
    n_hot = hidx_col.shape[0]
    pick_hot = hit(iota((n_hot, n_tok), 1), hidx_col[...])
    hown[0:n_hot] = dot(pick_hot, tok[...]).astype(BF)
    hown[n_hot:] = (hgate[...] * dot(pick_hot, cot[...])).astype(BF)
    hxs[me] = hown[...]
    hw[z, x] = hw_in[...]

    rr, rc = routes_row[...], routes_col[...]
    onehot = hit(iota((NZ * NX, n_tok), 0), rr)
    ahead = jnp.where(iota((n_tok, n_tok), 0) < iota((n_tok, n_tok), 1), 1.0, 0.0).astype(BF)
    pos_r = jnp.sum(dot(onehot, ahead) * onehot.astype(F32), axis=0, keepdims=True).astype(jnp.int32)
    onehot = hit(iota((n_tok, n_tok), 1), rc)
    ahead = jnp.where(iota((n_tok, n_tok), 1) < iota((n_tok, n_tok), 0), 1.0, 0.0).astype(BF)
    pos_c = jnp.sum(dot(ahead, onehot) * onehot.astype(F32), axis=1, keepdims=True).astype(jnp.int32)

    def tail_code(route, pos, i):
        high = jnp.where(pos >= 3, 1, 0)
        return jnp.where(pos - 3 * high == i, route * MSG + 12 + high, -9)

    rows = NZ * NX * MSG
    q_id = iota((rows, n_tok), 0)
    main_x = hit(q_id, rr * MSG + pos_r)
    main_s = hit(q_id, rr * MSG + pos_r + CAP)

    def columns(k, size):
        part = slice(k, k + size)
        return tok[:, part], (gates[...] * cot[:, part].astype(F32)).astype(BF)

    tail_x, tail_s = columns(3 * third, third)
    for i in range(3):
        code = tail_code(rr, pos_r, i)
        choose = jnp.concatenate([main_x, main_s, hit(q_id, code), hit(q_id, code + 2)], axis=1)
        part_x, part_s = columns(i * third, third)
        data = jnp.concatenate([part_x, part_s, tail_x, tail_s], axis=0)
        msend[:, :, i * third : (i + 1) * third] = (
            dot(choose, data).astype(BF).reshape(NZ * NX, MSG, third)
        )
    mrecv[e] = msend[e]

    pl.semaphore_wait(barrier, NZ * NX + 2)

    halves = {
        "h": (hown, hxs, hxs.shape[1] // 2),
        "g": (wgu_in.at[0], wgu, wgu.shape[1] // 2),
        "d": (wdn_in.at[0], wdn, wdn.shape[1] // 2),
    }

    def half(name, block, k):
        size = halves[name][2]
        return halves[name][1].at[block, pl.ds(k * size, size)]

    def own_half(name, k):
        size = halves[name][2]
        return halves[name][0].at[pl.ds(k * size, size)]

    def ring_start(names):
        for k in (0, 1):
            for name in names:
                send((name, "up", k), own_half(name, k), half(name, me, k), up)
                send((name, "down", 1 - k), own_half(name, 1 - k), half(name, me, 1 - k), down)
        for name in names:
            send((name, "mate"), halves[name][0], halves[name][1].at[me], mate)

    def ring_near(names, k):
        for name in names:
            low, high = half(name, 2 * ym + c, k), half(name, 2 * yp + c, 1 - k)
            arrived((name, "up", k), low)
            if k == 0:
                send((name, "up", 2), low, low, up)
            send((name, "mate", 0, k), low, low, mate)
            arrived((name, "down", 1 - k), high)
            if k == 0:
                send((name, "down", 2), high, high, down)
            send((name, "mate", 1, k), high, high, mate)

    def ring_far(names):
        for name in names:
            low, high = half(name, 2 * y2 + c, 0), half(name, 2 * y2 + c, 1)
            arrived((name, "up", 2), low)
            send((name, "mate", 2, 0), low, low, mate)
            arrived((name, "down", 2), high)
            send((name, "mate", 2, 1), high, high, mate)

    def ring_end(names):
        d = 1 - c
        for name in names:
            arrived((name, "mate"), halves[name][1].at[2 * y + d])
            for k in (0, 1):
                arrived((name, "mate", 0, k), half(name, 2 * ym + d, k))
                arrived((name, "mate", 1, k), half(name, 2 * yp + d, 1 - k))
                arrived((name, "mate", 2, k), half(name, 2 * y2 + d, k))

    ring_start(["h"])
    for j in range(1, NZ):
        send(("hz", j), hw_in, hw.at[z, x], (me, NX * ((z + j) % NZ) + x))

    def token_copy(j, sign, out_ref, in_ref, s, r):
        peer = (e + j) % (NZ * NX) if sign else (e + NZ * NX - j) % (NZ * NX)
        return pltpu.make_async_remote_copy(
            src_ref=out_ref.at[peer] if sign else in_ref.at[peer],
            dst_ref=in_ref.at[e] if sign else in_ref.at[peer],
            send_sem=s.at[j],
            recv_sem=r.at[j],
            device_id=(me, peer),
            device_id_type=MESH,
        )

    ring_start(["g", "d"])

    @pl.loop(1, NZ * NX)
    def _(j):
        token_copy(j, True, msend, mrecv, a_s, a_r).start()

    ring_near(["h"], 0)
    ring_near(["h"], 1)

    for j in range(1, NZ):
        arrived(("hz", j), hw.at[(z + NZ - j) % NZ, x])

    def hw_half(col, k):
        return hw.at[pl.ds(k * (NZ // 2), NZ // 2), col]

    for k in (0, 1):
        send(("x", "right", k), hw_half(x, k), hw_half(x, k), right)
        send(("x", "left", 1 - k), hw_half(x, 1 - k), hw_half(x, 1 - k), left)
    ring_far(["h"])
    ring_near(["g", "d"], 0)
    arrived(("x", "right", 0), hw_half(xm, 0))
    send(("x", "right", 2), hw_half(xm, 0), hw_half(xm, 0), right)
    arrived(("x", "left", 1), hw_half(xp, 1))
    send(("x", "left", 2), hw_half(xp, 1), hw_half(xp, 1), left)
    arrived(("x", "right", 1), hw_half(xm, 1))
    arrived(("x", "left", 0), hw_half(xp, 0))
    arrived(("x", "right", 2), hw_half(x2, 0))
    arrived(("x", "left", 2), hw_half(x2, 1))
    ring_end(["h"])
    own_gu.wait()
    own_dn.wait()

    n_dp = hxs.shape[0]
    n_all = n_dp * n_hot
    hot_x = hxs[:, 0:n_hot, :].reshape(n_all, width)
    hot_s = hxs[:, n_hot:, :].reshape(n_all, width)
    act = dot(hot_x, hw[:, :, :, 0:256].reshape(width, 256))
    hot_g, hot_u = act[:, 0:128], act[:, 128:256]
    hot_dh = dot(hot_s, hw[:, :, :, 256:384].reshape(width, 128))
    sigma = 1.0 / (1.0 + jnp.exp(-hot_g))
    hot_h = (hot_g * sigma * hot_u).astype(BF)
    hot_d = jnp.concatenate(
        [
            (hot_dh * hot_u * sigma * (1.0 + hot_g * (1.0 - sigma))).astype(BF),
            (hot_dh * hot_g * sigma).astype(BF),
        ],
        axis=1,
    )
    quarter = width // 4
    for k in range(4):
        part = slice(k * quarter, (k + 1) * quarter)
        zs = slice(2 * k, 2 * k + 2)
        w_gu = hw[zs, :, :, 0:256].reshape(quarter, 256)
        w_dn = hw[zs, :, :, 256:384].reshape(quarter, 128)
        phb[:, 0:n_hot, part] = dot_nt(hot_h, w_dn).astype(BF).reshape(n_dp, n_hot, quarter)
        phb[:, n_hot:, part] = dot_nt(hot_d, w_gu).astype(BF).reshape(n_dp, n_hot, quarter)
        x_t = hxs[:, 0:n_hot, part].reshape(n_all, quarter).T
        s_t = hxs[:, n_hot:, part].reshape(n_all, quarter).T
        block = (2, NX, hw.shape[2])
        hg[zs, :, :, 0:256] = dot(x_t, hot_d).astype(BF).reshape(*block, 256)
        hg[zs, :, :, 256:384] = dot(s_t, hot_h).astype(BF).reshape(*block, 128)

    sums = {
        "h": (phb, qhb, rhb, hxs.shape[1] // 2, 32),
        "g": (pgu, qgu, rgu, wgu.shape[1] // 2, 32),
        "d": (pdn, qdn, rdn, wdn.shape[1] // 2, 48),
    }

    def chip_send(name, yy):
        p, q = sums[name][0:2]
        send((name, "chip", (yy,)), p.at[2 * CHIP[yy] + 1 - c], q.at[CHIP[yy]], mate)

    CHIP = {"y": y, "p": yp, "m": ym, "2": y2}

    def chip_add(name, yy):
        p, q, _, size, step = sums[name]
        arrived((name, "chip", (yy,)), q.at[CHIP[yy]])

        @pl.loop(0, 2 * size // step)
        def _(i):
            part = pl.ds(pl.multiple_of(i * step, step), step)
            q[CHIP[yy], part] = (
                q[CHIP[yy], part].astype(F32) + p[2 * CHIP[yy] + c, part].astype(F32)
            ).astype(BF)

    def q_half(name, yy, k):
        size = sums[name][3]
        return sums[name][1].at[CHIP[yy], pl.ds(k * size, size)]

    def r_half(name, slot, k):
        size = sums[name][3]
        return sums[name][2].at[slot, pl.ds(k * size, size)]

    def far_send(name):
        send((name, "far", 0), q_half(name, "2", 0), r_half(name, 0, 0), up)
        send((name, "far", 1), q_half(name, "2", 1), r_half(name, 0, 1), down)

    def near_send(name, first):
        if first:
            send((name, "sum", 0), q_half(name, "p", 1), r_half(name, 1, 1), up)
            send((name, "sum", 1), q_half(name, "m", 0), r_half(name, 2, 0), down)
        else:
            send((name, "sum", 2), q_half(name, "p", 0), r_half(name, 1, 0), up)
            send((name, "sum", 3), q_half(name, "m", 1), r_half(name, 2, 1), down)

    def near_add(name):
        _, q, r, size, step = sums[name]
        step = min(step, size)
        for k, yy in ((0, "p"), (1, "m")):
            arrived((name, "far", k), r_half(name, 0, k))

            @pl.loop(0, size // step)
            def _(i):
                part = pl.ds(pl.multiple_of(k * size + i * step, 16), step)
                q[CHIP[yy], part] = (
                    q[CHIP[yy], part].astype(F32) + r[0, part].astype(F32)
                ).astype(BF)

    def sum_wait(name):
        arrived((name, "sum", 0), r_half(name, 1, 1))
        arrived((name, "sum", 1), r_half(name, 2, 0))
        arrived((name, "sum", 2), r_half(name, 1, 0))
        arrived((name, "sum", 3), r_half(name, 2, 1))

    for yy in "2pmy":
        chip_send("h", yy)

    def hg_half(col, k):
        return hg.at[pl.ds(k * (NZ // 2), NZ // 2), col]

    def hgr_half(slot, k):
        return hgr.at[slot, pl.ds(k * (NZ // 2), NZ // 2)]

    send(("gx", "far", 0), hg_half(x2, 0), hgr_half(0, 0), right)
    send(("gx", "far", 1), hg_half(x2, 1), hgr_half(0, 1), left)
    send(("gx", "sum", 0), hg_half(xp, 1), hgr_half(1, 1), right)
    send(("gx", "sum", 1), hg_half(xm, 0), hgr_half(2, 0), left)

    ring_near(["g", "d"], 1)
    for yy in "2pmy":
        chip_add("h", yy)
    far_send("h")
    near_send("h", True)

    @pl.loop(1, NZ * NX)
    def _(j):
        token_copy(j, False, msend, mrecv, a_s, a_r).wait_recv()

    n_row = rxs.shape[0] // 2
    col_id = iota((2 * n_row, rows), 1)
    straight = hit(col_id, perm_col[:, 0:1])
    tail = None
    for i in range(3):
        part = mrecv[:, :, i * third : (i + 1) * third].reshape(rows, third)
        rxs[:, i * third : (i + 1) * third] = dot(straight, part).astype(BF)
        piece = dot(hit(col_id, perm_col[:, i + 1 : i + 2]), part)
        tail = piece if tail is None else tail + piece
    rxs[:, 3 * third :] = tail.astype(BF)
    for k in range(4):
        part = slice(k * third, (k + 1) * third)
        xt[part] = rxs[0:n_row, part].T

    arrived(("gx", "far", 0), hgr_half(0, 0))
    arrived(("gx", "far", 1), hgr_half(0, 1))
    for k, col in ((0, xp), (1, xm)):
        for i in range(NZ // 2):
            n = k * (NZ // 2) + i
            hg[n, col] = (hg[n, col].astype(F32) + hgr[0, n].astype(F32)).astype(BF)
    send(("gx", "sum", 2), hg_half(xp, 0), hgr_half(1, 0), right)
    send(("gx", "sum", 3), hg_half(xm, 1), hgr_half(2, 1), left)

    ring_far(["g", "d"])
    arrived(("gx", "sum", 0), hgr_half(1, 1))
    arrived(("gx", "sum", 1), hgr_half(2, 0))
    arrived(("gx", "sum", 2), hgr_half(1, 0))
    arrived(("gx", "sum", 3), hgr_half(2, 1))
    for n in range(NZ):
        hg[n, x] = (
            hg[n, x].astype(F32) + hgr[1, n].astype(F32) + hgr[2, n].astype(F32)
        ).astype(BF)
    hgz[z] = hg[z, x]
    for j in range(1, NZ):
        there = (z + j) % NZ
        send(("gz", j), hg.at[there, x], hgz.at[z], (me, NX * there + x))
    near_add("h")
    near_send("h", False)
    ring_end(["g", "d"])

    hidden = wdn.shape[0] * wdn.shape[1]
    model = wgu.shape[0] * wgu.shape[1]
    w_dn2 = wdn.reshape(hidden, width)

    @pl.loop(0, hidden // 256)
    def _(n):
        first = pl.ds(pl.multiple_of(n * 256, 256), 256)
        second = pl.ds(pl.multiple_of(hidden + n * 256, 256), 256)
        g = dot(rxs[0:n_row], wgu[:, :, first].reshape(model, 256))
        u = dot(rxs[0:n_row], wgu[:, :, second].reshape(model, 256))
        dh = dot_nt(rxs[n_row:], w_dn2[first])
        s = 1.0 / (1.0 + jnp.exp(-g))
        h = (g * s * u).astype(BF)
        hid[:, first] = h
        ht[first] = h.T
        dact[:, first] = (dh * u * s * (1.0 + g * (1.0 - s))).astype(BF)
        dact[:, second] = (dh * g * s).astype(BF)

    half_rows = wgu.shape[1]

    def grad_gu(yy):
        lhs = xt[pl.ds(pl.multiple_of(CHIP[yy] * 2 * half_rows, 16), 2 * half_rows)]

        @pl.loop(0, 2 * hidden // 256)
        def _(n):
            part = pl.ds(pl.multiple_of(n * 256, 256), 256)
            both = dot(lhs, dact[:, part]).astype(BF)
            pgu[pl.ds(2 * CHIP[yy], 2), :, part] = both.reshape(2, half_rows, 256)

        chip_send("g", yy)

    grad_gu("2")

    @pl.loop(0, width // 256)
    def _(n):
        part = pl.ds(pl.multiple_of(n * 256, 256), 256)
        pdn[:, :, part] = dot(ht[...], rxs[n_row:, part]).astype(BF).reshape(*pdn.shape[0:2], 256)

    for yy in "2pmy":
        chip_send("d", yy)
    for name in "gd":
        chip_add(name, "2")
        far_send(name)

    @pl.loop(0, width // 256)
    def _(n):
        part = pl.ds(pl.multiple_of(n * 256, 256), 256)
        rxs[0:n_row, part] = dot(hid[...], w_dn2[:, part]).astype(BF)

    for k in range(wgu.shape[0] // 2):
        w = wgu[2 * k : 2 * k + 2].reshape(2 * half_rows, 2 * hidden)
        rxs[n_row:, k * 2 * half_rows : (k + 1) * 2 * half_rows] = dot_nt(dact[...], w).astype(BF)

    @pl.loop(1, NZ * NX)
    def _(j):
        token_copy(j, True, msend, mrecv, a_s, a_r).wait_send()

    row_id = iota((rows, 2 * n_row), 0)
    straight = hit(row_id, perm_row[0:1])
    for i in range(3):
        part = slice(i * third, (i + 1) * third)
        mixed = dot(straight, rxs[:, part]) + dot(
            hit(row_id, perm_row[i + 1 : i + 2]), rxs[:, 3 * third :]
        )
        msend[:, :, part] = mixed.astype(BF).reshape(NZ * NX, MSG, third)
    mback[e] = msend[e]

    @pl.loop(1, NZ * NX)
    def _(j):
        token_copy(j, True, msend, mback, b_s, b_r).start()

    grad_gu("p")
    grad_gu("m")
    for yy in "pm":
        for name in "gd":
            chip_add(name, yy)
    for name in "gd":
        near_send(name, True)
    grad_gu("y")
    for name in "gd":
        near_add(name)
        near_send(name, False)
    for name in "gd":
        chip_add(name, "y")

    total = hgz[z].astype(F32)
    for j in range(1, NZ):
        there = (z + NZ - j) % NZ
        arrived(("gz", j), hgz.at[there])
        total = total + hgz[there].astype(F32)
    scale = 1.0 / 32.0
    ghw_out[...] = (total * scale).astype(BF)

    sum_wait("h")
    hot_sum = qhb[y].astype(F32) + rhb[1].astype(F32) + rhb[2].astype(F32)
    back = jnp.concatenate([hgate[...] * hot_sum[0:n_hot], hot_sum[n_hot:]], axis=1)
    upper = back.astype(BF)
    back = jnp.concatenate([upper, (back - upper.astype(F32)).astype(BF)], axis=0)
    spread = hit(iota((n_tok, 2 * n_hot), 0), hidx_row[...])

    @pl.loop(1, NZ * NX)
    def _(j):
        token_copy(j, False, msend, mback, b_s, b_r).wait_recv()

    lane_id = iota((n_tok, rows), 1)
    code = rc * MSG + pos_c
    straight = jnp.concatenate([hit(lane_id, code), hit(lane_id, code + CAP)], axis=0)
    tail = None
    for i in range(4):
        part = slice(i * third, (i + 1) * third)
        if i < 3:
            data = mback[:, :, part].reshape(rows, third)
            got = dot(straight, data)
            code = tail_code(rc, pos_c, i)
            piece = dot(
                jnp.concatenate([hit(lane_id, code), hit(lane_id, code + 2)], axis=0), data
            )
            tail = piece if tail is None else tail + piece
        else:
            got = tail
        hot_part = dot(spread, back[:, part])
        hot_grad = dot(spread, back[:, width + i * third : width + (i + 1) * third])
        lo_out[:, part] = (gates[...] * got[0:n_tok] + hot_part).astype(BF)
        ig_out[:, part] = (got[n_tok:] + hot_grad).astype(BF)

    for name, out in (("g", ggu_out), ("d", gdn_out)):
        _, q, r, size, step = sums[name]
        sum_wait(name)

        @pl.loop(0, 2 * size // step)
        def _(i):
            part = pl.ds(pl.multiple_of(i * step, step), step)
            value = q[y, part].astype(F32) + r[1, part].astype(F32) + r[2, part].astype(F32)
            out[0, part] = (value * scale).astype(BF)

    for copy in started:
        copy.wait_send()

    @pl.loop(1, NZ * NX)
    def _(j):
        token_copy(j, True, msend, mback, b_s, b_r).wait_send()


def row_tables(n_expert, n_row):
    table = np.full((4, 2 * n_row), -1, np.int32)
    for k in range(2):
        for p in range(n_expert):
            for r in range(CAP):
                n = k * n_row + p * CAP + r
                table[0, n] = p * MSG + k * CAP + r
                place = k * CAP + r
                table[1 + place % 3, n] = p * MSG + 12 + place // 3
    return table


def local(
    tokens, cotangent, routes, gates, hot_index, hot_gate, w_gate_up, w_down, w_hot_gu, w_hot_dn
):
    n_dp, n_e = lax.axis_size("dp"), lax.axis_size("expert")
    n_tok, width = tokens.shape
    n_hot = hot_index.shape[0]
    rows_gu, double = w_gate_up.shape[1:]
    rows_dn = w_down.shape[1]
    units, features = w_hot_dn.shape
    n_row = 256
    table = row_tables(n_e, n_row)
    perm_row = jnp.asarray(np.concatenate([table, np.full_like(table, -1)], axis=0))
    perm_col = jnp.asarray(np.pad(table.T, ((0, 0), (0, 124)), constant_values=-1))
    hot_w = jnp.concatenate([w_hot_gu, w_hot_dn[None]], axis=0)
    hot_w = jnp.pad(hot_w, ((0, 0), (0, 128 - units), (0, 0))).transpose(2, 0, 1)
    hot_w = hot_w.reshape(features, 384)
    vmem = pl.BlockSpec(memory_space=pltpu.VMEM)
    any_space = pl.BlockSpec(memory_space=pl.ANY)
    msg = (n_e, MSG, 3 * width // 4)
    hot2 = 2 * n_hot
    dma = pltpu.SemaphoreType.DMA
    outs = pl.pallas_call(
        kernel,
        out_shape=(
            jax.ShapeDtypeStruct((n_tok, width), BF),
            jax.ShapeDtypeStruct((n_tok, width), BF),
            jax.ShapeDtypeStruct(w_gate_up.shape, BF),
            jax.ShapeDtypeStruct(w_down.shape, BF),
            jax.ShapeDtypeStruct(hot_w.shape, BF),
        ),
        in_specs=[vmem] * 10 + [any_space] * 2 + [vmem],
        out_specs=(vmem,) * 5,
        scratch_shapes=[
            pltpu.VMEM((n_dp, rows_gu, double), BF),
            pltpu.VMEM((n_dp, rows_dn, width), BF),
            pltpu.VMEM((n_dp, hot2, width), BF),
            pltpu.VMEM((NZ, NX, features, 384), BF),
            pltpu.VMEM(msg, BF),
            pltpu.VMEM(msg, BF),
            pltpu.VMEM(msg, BF),
            pltpu.VMEM((2 * n_row, width), BF),
            pltpu.VMEM((width, n_row), BF),
            pltpu.VMEM((double // 2, n_row), BF),
            pltpu.VMEM((n_row, double // 2), BF),
            pltpu.VMEM((n_row, double), BF),
            pltpu.VMEM((n_dp, rows_gu, double), BF),
            pltpu.VMEM((n_dp, rows_dn, width), BF),
            pltpu.VMEM((n_dp, hot2, width), BF),
            pltpu.VMEM((NY, rows_gu, double), BF),
            pltpu.VMEM((NY, rows_dn, width), BF),
            pltpu.VMEM((NY, hot2, width), BF),
            pltpu.VMEM((3, rows_gu, double), BF),
            pltpu.VMEM((3, rows_dn, width), BF),
            pltpu.VMEM((3, hot2, width), BF),
            pltpu.VMEM((hot2, width), BF),
            pltpu.VMEM((NZ, NX, features, 384), BF),
            pltpu.VMEM((3, NZ, features, 384), BF),
            pltpu.VMEM((NZ, features, 384), BF),
            dma((112,)),
            dma((112,)),
            dma((n_e,)),
            dma((n_e,)),
            dma((n_e,)),
            dma((n_e,)),
            dma((2,)),
        ],
        compiler_params=pltpu.CompilerParams(
            collective_id=0, has_side_effects=True, vmem_limit_bytes=67043328
        ),
        name="expert_layer",
    )(
        tokens, cotangent, routes.reshape(1, n_tok), routes, gates,
        jnp.tile(hot_index, 2).reshape(1, hot2), hot_index.reshape(n_hot, 1),
        hot_gate.reshape(n_hot, 1), perm_col, perm_row, w_gate_up, w_down, hot_w,
    )
    layer_out, input_grad, grad_gu, grad_dn, grad_hot = outs
    grad_hot = grad_hot.reshape(features, 3, 128)[:, :, :units].transpose(1, 2, 0)
    return layer_out, input_grad, grad_gu, grad_dn, grad_hot[0:2], grad_hot[2]


def solution(mesh):
    placed = (
        P(("dp", "expert"), None),
        P(("dp", "expert"), None),
        P(("dp", "expert"), None),
        P(("dp", "expert"), None),
        P(("dp", "expert")),
        P(("dp", "expert")),
        P("expert", "dp", None),
        P("expert", "dp", None),
        P(None, "dp", "expert"),
        P("dp", "expert"),
    )
    return jax.shard_map(
        local,
        mesh=mesh,
        in_specs=placed,
        out_specs=(
            P(("dp", "expert"), None),
            P(("dp", "expert"), None),
            P("expert", "dp", None),
            P("expert", "dp", None),
            P(None, "dp", "expert"),
            P("dp", "expert"),
        ),
        check_vma=False,
    )
```

```python
import functools

import jax
import jax.numpy as jnp
from jax import lax
from jax.experimental import pallas as pl
from jax.experimental.pallas import tpu as pltpu
from jax.sharding import PartitionSpec as P

MESH = pl.DeviceIdType.MESH
BF = jnp.bfloat16
F32 = jnp.float32
CAP = 6
MSG = 8
NZ, NX, NY = 8, 4, 4


def dot(a, b):
    return jnp.dot(a, b, preferred_element_type=F32)


def dot_nt(a, b):
    return lax.dot_general(a, b, (((1,), (1,)), ((), ())), preferred_element_type=F32)


def hit(a, b):
    return jnp.where(a == b, 1.0, 0.0).astype(BF)


def iota(shape, axis):
    return lax.broadcasted_iota(jnp.int32, shape, axis)


class Sems:
    def __init__(self, send, recv):
        self.send, self.recv, self.ids = send, recv, {}

    def __call__(self, name):
        if name not in self.ids:
            self.ids[name] = len(self.ids)
        n = self.ids[name]
        return self.send.at[n], self.recv.at[n]


def kernel(
    tok_in, cot_in, wgu_in, wdn_in,
    routes_row, gates_row, hidx_row, hgate_row, hot_gu_in, hot_dn_in,
    lo_out, ig_out, ggu_out, gdn_out, ghg_out, ghd_out,
    tok, cot, hw_in, lo_buf, ig_buf, ghg_buf, gates, hgate,
    wgu, wdn, hxs, hw, send_x, send_s, recv_x, recv_s, back_o, back_g, rx, rs, xt, ht, hid, dact, acc, dh_acc,
    pgu, pdn, phb, qgu, qdn, qhb, rgu, rdn, rhb, hown, hg, hgr, hgz,
    sem_s, sem_r, x_s, x_r, s_s, s_r, o_s, o_r, g_s, g_r, loc,
):
    me, e = lax.axis_index("dp"), lax.axis_index("expert")
    y, c = me // 2, me % 2
    z, x = e // NX, e % NX
    yp, ym, y2 = (y + 1) % NY, (y + 3) % NY, (y + 2) % NY
    xp, xm, x2 = (x + 1) % NX, (x + 3) % NX, (x + 2) % NX
    up, down, mate = (2 * yp + c, e), (2 * ym + c, e), (2 * y + 1 - c, e)
    right, left = (me, NX * z + xp), (me, NX * z + xm)
    sems = Sems(sem_s, sem_r)
    started = []

    def send(name, src, dst, dev):
        s, r = sems(name)
        copy = pltpu.make_async_remote_copy(
            src_ref=src, dst_ref=dst, send_sem=s, recv_sem=r, device_id=dev, device_id_type=MESH
        )
        copy.start()
        started.append(copy)

    def arrived(name, dst):
        s, r = sems(name)
        pltpu.make_async_remote_copy(
            src_ref=dst, dst_ref=dst, send_sem=s, recv_sem=r, device_id=mate, device_id_type=MESH
        ).wait_recv()

    barrier = pltpu.get_barrier_semaphore()
    for dev in (up, down, mate):
        pl.semaphore_signal(barrier, inc=1, device_id=dev, device_id_type=MESH)

    @pl.loop(1, NZ * NX)
    def _(j):
        pl.semaphore_signal(
            barrier, inc=1, device_id=(me, (e + j) % (NZ * NX)), device_id_type=MESH
        )

    def fetch(n, src, dst):
        copy = pltpu.make_async_copy(src, dst, loc.at[n])
        copy.start()
        return copy

    rows_in = (fetch(0, tok_in, tok), fetch(1, cot_in, cot))
    later_in = (
        fetch(2, wgu_in.at[0], wgu.at[me]),
        fetch(3, wdn_in.at[0], wdn.at[me]),
    )

    n_tok, width = tok.shape
    third = 3 * width // 4 // 3
    n_hot = hidx_row.shape[1]

    def turned(row):
        n = row.shape[1]
        return jnp.sum(jnp.where(iota((n, n), 0) == iota((n, n), 1), row, 0.0), axis=1, keepdims=True)

    rr = routes_row[...]
    rc = turned(rr.astype(F32)).astype(jnp.int32)
    gates[...] = turned(gates_row[...])
    hgate[...] = turned(hgate_row[...])
    hidx_col = turned(hidx_row[...].astype(F32)).astype(jnp.int32)
    units = hot_dn_in.shape[1]
    zeros = jnp.zeros((hw_in.shape[0], 128 - units), BF)
    for n, w in enumerate((hot_gu_in[0], hot_gu_in[1], hot_dn_in[...])):
        hw_in[:, n * 128 : (n + 1) * 128] = jnp.concatenate([w, zeros], axis=1)

    for copy in rows_in:
        copy.wait()
    pick_hot = hit(iota((n_hot, n_tok), 1), hidx_col)
    hown[0:n_hot] = dot(pick_hot, tok[...]).astype(BF)
    hown[n_hot:] = (hgate[...] * dot(pick_hot, cot[...])).astype(BF)
    hxs[me] = hown[...]
    hw[z, x] = hw_in[...]

    onehot = hit(iota((NZ * NX, n_tok), 0), rr)
    ahead = jnp.where(iota((n_tok, n_tok), 0) < iota((n_tok, n_tok), 1), 1.0, 0.0).astype(BF)
    pos_r = jnp.sum(dot(onehot, ahead) * onehot.astype(F32), axis=0, keepdims=True).astype(jnp.int32)
    onehot = hit(iota((n_tok, n_tok), 1), rc)
    ahead = jnp.where(iota((n_tok, n_tok), 1) < iota((n_tok, n_tok), 0), 1.0, 0.0).astype(BF)
    pos_c = jnp.sum(dot(ahead, onehot) * onehot.astype(F32), axis=1, keepdims=True).astype(jnp.int32)

    def tail_code(route, pos, i):
        high = jnp.where(pos >= 3, 1, 0)
        return jnp.where(pos - 3 * high == i, route * MSG + CAP + high, -9)

    rows = NZ * NX * MSG
    q_id = iota((rows, n_tok), 0)
    main = hit(q_id, rr * MSG + pos_r)

    def columns(i):
        part = slice(i * third, (i + 1) * third)
        return tok[:, part], (gates[...] * cot[:, part].astype(F32)).astype(BF)

    tails = columns(3)
    for i in range(3):
        choose = jnp.concatenate([main, hit(q_id, tail_code(rr, pos_r, i))], axis=1)
        for out, now, tail in zip((send_x, send_s), columns(i), tails):
            data = dot(choose, jnp.concatenate([now, tail], axis=0))
            out[:, :, i * third : (i + 1) * third] = data.astype(BF).reshape(NZ * NX, MSG, third)
    recv_x[e] = send_x[e]
    recv_s[e] = send_s[e]

    pl.semaphore_wait(barrier, NZ * NX + 2)

    halves = {
        "h": (hown, hxs, hxs.shape[1] // 2),
        "g": (wgu_in.at[0], wgu, wgu.shape[1] // 2),
        "d": (wdn_in.at[0], wdn, wdn.shape[1] // 2),
    }

    def half(name, block, k):
        size = halves[name][2]
        return halves[name][1].at[block, pl.ds(k * size, size)]

    def own_half(name, k):
        size = halves[name][2]
        return halves[name][0].at[pl.ds(k * size, size)]

    def ring_start(names):
        for k in (0, 1):
            for name in names:
                send((name, "up", k), own_half(name, k), half(name, me, k), up)
                send((name, "down", 1 - k), own_half(name, 1 - k), half(name, me, 1 - k), down)
        for name in names:
            send((name, "mate"), halves[name][0], halves[name][1].at[me], mate)

    def ring_near(names, k):
        for name in names:
            low, high = half(name, 2 * ym + c, k), half(name, 2 * yp + c, 1 - k)
            arrived((name, "up", k), low)
            if k == 0:
                send((name, "up", 2), low, low, up)
            send((name, "mate", 0, k), low, low, mate)
            arrived((name, "down", 1 - k), high)
            if k == 0:
                send((name, "down", 2), high, high, down)
            send((name, "mate", 1, k), high, high, mate)

    def ring_far(names):
        for name in names:
            low, high = half(name, 2 * y2 + c, 0), half(name, 2 * y2 + c, 1)
            arrived((name, "up", 2), low)
            send((name, "mate", 2, 0), low, low, mate)
            arrived((name, "down", 2), high)
            send((name, "mate", 2, 1), high, high, mate)

    def ring_end(names, near=True, far=True):
        d = 1 - c
        for name in names:
            if near:
                arrived((name, "mate"), halves[name][1].at[2 * y + d])
            for k in (0, 1):
                if near:
                    arrived((name, "mate", 0, k), half(name, 2 * ym + d, k))
                    arrived((name, "mate", 1, k), half(name, 2 * yp + d, 1 - k))
                if far:
                    arrived((name, "mate", 2, k), half(name, 2 * y2 + d, k))

    ring_start(["h"])
    for j in range(1, NZ):
        send(("hz", j), hw_in, hw.at[z, x], (me, NX * ((z + j) % NZ) + x))

    def token_copy(j, sign, out_ref, in_ref, s, r):
        peer = (e + j) % (NZ * NX) if sign else (e + NZ * NX - j) % (NZ * NX)
        return pltpu.make_async_remote_copy(
            src_ref=out_ref.at[peer] if sign else in_ref.at[peer],
            dst_ref=in_ref.at[e] if sign else in_ref.at[peer],
            send_sem=s.at[j],
            recv_sem=r.at[j],
            device_id=(me, peer),
            device_id_type=MESH,
        )

    def tokens_start(*copy):
        @pl.loop(1, NZ * NX)
        def _(j):
            token_copy(j, True, *copy).start()

    def tokens_wait(*copy):
        @pl.loop(1, NZ * NX)
        def _(j):
            token_copy(j, False, *copy).wait_recv()

    def tokens_sent(*copy):
        @pl.loop(1, NZ * NX)
        def _(j):
            token_copy(j, True, *copy).wait_send()

    ring_start(["d", "g"])
    tokens_start(send_x, recv_x, x_s, x_r)
    tokens_start(send_s, recv_s, s_s, s_r)

    ring_near(["h"], 0)
    ring_near(["h"], 1)

    for j in range(1, NZ):
        arrived(("hz", j), hw.at[(z + NZ - j) % NZ, x])

    def hw_half(col, k):
        return hw.at[pl.ds(k * (NZ // 2), NZ // 2), col]

    for k in (0, 1):
        send(("x", "right", k), hw_half(x, k), hw_half(x, k), right)
        send(("x", "left", 1 - k), hw_half(x, 1 - k), hw_half(x, 1 - k), left)

    ring_far(["h"])
    ring_near(["d", "g"], 0)
    arrived(("x", "right", 0), hw_half(xm, 0))
    send(("x", "right", 2), hw_half(xm, 0), hw_half(xm, 0), right)
    arrived(("x", "left", 1), hw_half(xp, 1))
    send(("x", "left", 2), hw_half(xp, 1), hw_half(xp, 1), left)
    arrived(("x", "right", 1), hw_half(xm, 1))
    arrived(("x", "left", 0), hw_half(xp, 0))
    arrived(("x", "right", 2), hw_half(x2, 0))
    arrived(("x", "left", 2), hw_half(x2, 1))
    ring_end(["h"])
    for copy in later_in:
        copy.wait()

    n_dp = hxs.shape[0]
    n_all = n_dp * n_hot
    hot_x = hxs[:, 0:n_hot, :].reshape(n_all, width)
    hot_s = hxs[:, n_hot:, :].reshape(n_all, width)
    act = dot(hot_x, hw[:, :, :, 0:256].reshape(width, 256))
    hot_g, hot_u = act[:, 0:128], act[:, 128:256]
    hot_dh = dot(hot_s, hw[:, :, :, 256:384].reshape(width, 128))
    sigma = 1.0 / (1.0 + jnp.exp(-hot_g))
    hot_h = (hot_g * sigma * hot_u).astype(BF)
    hot_d = jnp.concatenate(
        [
            (hot_dh * hot_u * sigma * (1.0 + hot_g * (1.0 - sigma))).astype(BF),
            (hot_dh * hot_g * sigma).astype(BF),
        ],
        axis=1,
    )
    quarter = width // 4
    for k in range(4):
        part = slice(k * quarter, (k + 1) * quarter)
        zs = slice(2 * k, 2 * k + 2)
        w_gu = hw[zs, :, :, 0:256].reshape(quarter, 256)
        w_dn = hw[zs, :, :, 256:384].reshape(quarter, 128)
        phb[:, 0:n_hot, part] = dot_nt(hot_h, w_dn).astype(BF).reshape(n_dp, n_hot, quarter)
        phb[:, n_hot:, part] = dot_nt(hot_d, w_gu).astype(BF).reshape(n_dp, n_hot, quarter)
        x_t = hxs[:, 0:n_hot, part].reshape(n_all, quarter).T
        s_t = hxs[:, n_hot:, part].reshape(n_all, quarter).T
        block = (2, NX, hw.shape[2])
        hg[zs, :, :, 0:256] = dot(x_t, hot_d).astype(BF).reshape(*block, 256)
        hg[zs, :, :, 256:384] = dot(s_t, hot_h).astype(BF).reshape(*block, 128)

    sums = {
        "h": (phb, qhb, rhb, hxs.shape[1] // 2, 32),
        "g": (pgu, qgu, rgu, wgu.shape[1] // 2, 32),
        "d": (pdn, qdn, rdn, wdn.shape[1] // 2, 48),
    }

    def chip_send(name, yy):
        p, q = sums[name][0:2]
        send((name, "chip", (yy,)), p.at[2 * CHIP[yy] + 1 - c], q.at[CHIP[yy]], mate)

    CHIP = {"y": y, "p": yp, "m": ym, "2": y2}

    def chip_add(name, yy):
        p, q, _, size, step = sums[name]
        arrived((name, "chip", (yy,)), q.at[CHIP[yy]])

        @pl.loop(0, 2 * size // step)
        def _(i):
            part = pl.ds(pl.multiple_of(i * step, step), step)
            q[CHIP[yy], part] = (
                q[CHIP[yy], part].astype(F32) + p[2 * CHIP[yy] + c, part].astype(F32)
            ).astype(BF)

    def q_half(name, yy, k):
        size = sums[name][3]
        return sums[name][1].at[CHIP[yy], pl.ds(k * size, size)]

    def r_half(name, slot, k):
        size = sums[name][3]
        return sums[name][2].at[slot, pl.ds(k * size, size)]

    def far_send(name):
        send((name, "far", 0), q_half(name, "2", 0), r_half(name, 0, 0), up)
        send((name, "far", 1), q_half(name, "2", 1), r_half(name, 0, 1), down)

    def near_send(name, first):
        if first:
            send((name, "sum", 0), q_half(name, "p", 1), r_half(name, 1, 1), up)
            send((name, "sum", 1), q_half(name, "m", 0), r_half(name, 2, 0), down)
        else:
            send((name, "sum", 2), q_half(name, "p", 0), r_half(name, 1, 0), up)
            send((name, "sum", 3), q_half(name, "m", 1), r_half(name, 2, 1), down)

    def near_add(name):
        _, q, r, size, step = sums[name]
        step = min(step, size)
        for k, yy in ((0, "p"), (1, "m")):
            arrived((name, "far", k), r_half(name, 0, k))

            @pl.loop(0, size // step)
            def _(i):
                part = pl.ds(pl.multiple_of(k * size + i * step, 16), step)
                q[CHIP[yy], part] = (
                    q[CHIP[yy], part].astype(F32) + r[0, part].astype(F32)
                ).astype(BF)

    def sum_wait(name):
        arrived((name, "sum", 0), r_half(name, 1, 1))
        arrived((name, "sum", 1), r_half(name, 2, 0))
        arrived((name, "sum", 2), r_half(name, 1, 0))
        arrived((name, "sum", 3), r_half(name, 2, 1))

    for yy in "2pmy":
        chip_send("h", yy)

    def hg_half(col, k):
        return hg.at[pl.ds(k * (NZ // 2), NZ // 2), col]

    def hgr_half(slot, k):
        return hgr.at[slot, pl.ds(k * (NZ // 2), NZ // 2)]

    send(("gx", "far", 0), hg_half(x2, 0), hgr_half(0, 0), right)
    send(("gx", "far", 1), hg_half(x2, 1), hgr_half(0, 1), left)
    send(("gx", "sum", 0), hg_half(xp, 1), hgr_half(1, 1), right)
    send(("gx", "sum", 1), hg_half(xm, 0), hgr_half(2, 0), left)

    ring_near(["d", "g"], 1)
    for yy in "2pmy":
        chip_add("h", yy)
    far_send("h")
    near_send("h", True)

    n_row = rows
    hidden = wdn.shape[0] * wdn.shape[1]
    w_dn2 = wdn.reshape(hidden, width)
    chip_rows = 2 * wgu.shape[1]
    row_id, col_id = iota((rows, rows), 0), iota((rows, rows), 1)
    kept = (iota((rows, 1), 0) & (MSG - 1)) < CAP

    def spread_tail(a, b, i):
        place = a & (MSG - 1)
        return hit(b, jnp.where(place < CAP, tail_code(a >> 3, place, i), -9))

    def rows_of(message, out):
        tail = None
        for i in range(3):
            part = slice(i * third, (i + 1) * third)
            data = message[:, :, part].reshape(rows, third)
            out[:, part] = jnp.where(kept, data, jnp.zeros_like(data))
            piece = dot(spread_tail(row_id, col_id, i), data)
            tail = piece if tail is None else tail + piece
        out[:, 3 * third :] = tail.astype(BF)

    def message_of(data, out):
        for i in range(3):
            part = slice(i * third, (i + 1) * third)
            moved = dot(spread_tail(col_id, row_id, i), data[:, 3 * third :])
            out[:, :, part] = (
                jnp.where(kept, data[:, part].astype(F32), moved).astype(BF).reshape(NZ * NX, MSG, third)
            )

    def act_block(yy, part):
        ks = pl.ds(pl.multiple_of(CHIP[yy] * chip_rows, 128), chip_rows)
        w = wgu[pl.ds(2 * CHIP[yy], 2), :, part].reshape(chip_rows, 256)
        return dot(rx[:, ks], w)

    tokens_wait(send_x, recv_x, x_s, x_r)
    rows_of(recv_x, rx)
    for k in range(4):
        part = slice(k * third, (k + 1) * third)
        xt[part] = rx[:, part].T
    ring_end(["d", "g"], far=False)

    @pl.loop(0, 2 * hidden // 256)
    def _(n):
        part = pl.ds(pl.multiple_of(n * 256, 256), 256)
        acc[:, part] = act_block("y", part) + act_block("m", part) + act_block("p", part)

    ring_far(["d"])
    tokens_wait(send_s, recv_s, s_s, s_r)
    rows_of(recv_s, rs)
    ring_far(["g"])
    ring_end(["d"], near=False)

    @pl.loop(0, hidden // 256)
    def _(n):
        part = pl.ds(pl.multiple_of(n * 256, 256), 256)
        dh_acc[:, part] = dot_nt(rs[...], w_dn2[part])

    ring_end(["g"], near=False)

    @pl.loop(0, hidden // 256)
    def _(n):
        first = pl.ds(pl.multiple_of(n * 256, 256), 256)
        second = pl.ds(pl.multiple_of(hidden + n * 256, 256), 256)
        g = acc[:, first] + act_block("2", first)
        u = acc[:, second] + act_block("2", second)
        dh = dh_acc[:, first]
        s = 1.0 / (1.0 + jnp.exp(-g))
        h = (g * s * u).astype(BF)
        hid[:, first] = h
        ht[first] = h.T
        dact[:, first] = (dh * u * s * (1.0 + g * (1.0 - s))).astype(BF)
        dact[:, second] = (dh * g * s).astype(BF)

    half_rows = wgu.shape[1]

    def grad_gu(yy):
        lhs = xt[pl.ds(pl.multiple_of(CHIP[yy] * 2 * half_rows, 16), 2 * half_rows)]

        @pl.loop(0, 2 * hidden // 256)
        def _(n):
            part = pl.ds(pl.multiple_of(n * 256, 256), 256)
            both = dot(lhs, dact[:, part]).astype(BF)
            pgu[pl.ds(2 * CHIP[yy], 2), :, part] = both.reshape(2, half_rows, 256)

        chip_send("g", yy)

    grad_gu("2")

    @pl.loop(0, width // 256)
    def _(n):
        part = pl.ds(pl.multiple_of(n * 256, 256), 256)
        pdn[:, :, part] = dot(ht[...], rs[:, part]).astype(BF).reshape(*pdn.shape[0:2], 256)

    for yy in "2pmy":
        chip_send("d", yy)
    for name in "gd":
        chip_add(name, "2")
        far_send(name)

    near_add("h")
    near_send("h", False)

    arrived(("gx", "far", 0), hgr_half(0, 0))
    arrived(("gx", "far", 1), hgr_half(0, 1))
    for k, col in ((0, xp), (1, xm)):
        for i in range(NZ // 2):
            n = k * (NZ // 2) + i
            hg[n, col] = (hg[n, col].astype(F32) + hgr[0, n].astype(F32)).astype(BF)
    send(("gx", "sum", 2), hg_half(xp, 0), hgr_half(1, 0), right)
    send(("gx", "sum", 3), hg_half(xm, 1), hgr_half(2, 1), left)


    @pl.loop(0, width // 256)
    def _(n):
        part = pl.ds(pl.multiple_of(n * 256, 256), 256)
        rx[:, part] = dot(hid[...], w_dn2[:, part]).astype(BF)

    tokens_sent(send_x, recv_x, x_s, x_r)
    message_of(rx, send_x)
    back_o[e] = send_x[e]
    tokens_start(send_x, back_o, o_s, o_r)
    grad_gu("p")
    grad_gu("m")
    for k in range(wgu.shape[0] // 2):
        w = wgu[2 * k : 2 * k + 2].reshape(chip_rows, 2 * hidden)
        rs[:, k * chip_rows : (k + 1) * chip_rows] = dot_nt(dact[...], w).astype(BF)
    tokens_sent(send_s, recv_s, s_s, s_r)
    message_of(rs, send_s)
    back_g[e] = send_s[e]
    tokens_start(send_s, back_g, g_s, g_r)
    for yy in "pm":
        for name in "gd":
            chip_add(name, yy)
    for name in "gd":
        near_send(name, True)
    for name in "gd":
        near_add(name)
        near_send(name, False)
    arrived(("gx", "sum", 0), hgr_half(1, 1))
    arrived(("gx", "sum", 1), hgr_half(2, 0))
    arrived(("gx", "sum", 2), hgr_half(1, 0))
    arrived(("gx", "sum", 3), hgr_half(2, 1))
    for n in range(NZ):
        hg[n, x] = (
            hg[n, x].astype(F32) + hgr[1, n].astype(F32) + hgr[2, n].astype(F32)
        ).astype(BF)
    hgz[z] = hg[z, x]
    for j in range(1, NZ):
        there = (z + j) % NZ
        send(("gz", j), hg.at[there, x], hgz.at[z], (me, NX * there + x))
    grad_gu("y")
    for name in "gd":
        chip_add(name, "y")

    leaving = []
    sum_wait("h")
    hot_sum = qhb[y].astype(F32) + rhb[1].astype(F32) + rhb[2].astype(F32)
    back = jnp.concatenate([hgate[...] * hot_sum[0:n_hot], hot_sum[n_hot:]], axis=1)
    upper = back.astype(BF)
    lower = (back - upper.astype(F32)).astype(BF)
    spread = hit(iota((n_tok, n_hot), 0), hidx_row[...])

    lane_id = iota((n_tok, rows), 1)
    straight = hit(lane_id, rc * MSG + pos_c)
    bent = [hit(lane_id, tail_code(rc, pos_c, i)) for i in range(3)]

    def results(back_ref, hot_first, out):
        tail = None
        for i in range(4):
            part = slice(i * third, (i + 1) * third)
            if i < 3:
                data = back_ref[:, :, part].reshape(rows, third)
                got = dot(straight, data)
                piece = dot(bent[i], data)
                tail = piece if tail is None else tail + piece
            else:
                got = tail
            lanes = slice(hot_first + i * third, hot_first + (i + 1) * third)
            hot_part = dot(spread, upper[:, lanes]) + dot(spread, lower[:, lanes])
            if hot_first == 0:
                got = gates[...] * got
            out[:, part] = (got + hot_part).astype(BF)

    tokens_wait(send_x, back_o, o_s, o_r)
    results(back_o, 0, lo_buf)
    leaving.append(fetch(6, lo_buf, lo_out))
    tokens_wait(send_s, back_g, g_s, g_r)
    results(back_g, width, ig_buf)
    leaving.append(fetch(7, ig_buf, ig_out))
    scale = 1.0 / 32.0
    total = hgz[z].astype(F32)
    for j in range(1, NZ):
        there = (z + NZ - j) % NZ
        arrived(("gz", j), hgz.at[there])
        total = total + hgz[there].astype(F32)
    total = (total * scale).astype(BF)
    ghg_buf[0] = total[:, 0:units]
    ghg_buf[1] = total[:, 128 : 128 + units]
    ghg_buf[2] = total[:, 256 : 256 + units]
    leaving.append(fetch(8, ghg_buf.at[0:2], ghg_out))
    leaving.append(fetch(9, ghg_buf.at[2], ghd_out))


    for n, (name, out) in enumerate((("g", ggu_out), ("d", gdn_out))):
        _, q, r, size, step = sums[name]
        sum_wait(name)

        @pl.loop(0, 2 * size // step)
        def _(i):
            part = pl.ds(pl.multiple_of(i * step, step), step)
            value = q[y, part].astype(F32) + r[1, part].astype(F32) + r[2, part].astype(F32)
            q[y, part] = (value * scale).astype(BF)

        leaving.append(fetch(n, q.at[y], out.at[0]))

    for copy in started:
        copy.wait_send()
    for copy in leaving:
        copy.wait()

    tokens_sent(send_x, back_o, o_s, o_r)
    tokens_sent(send_s, back_g, g_s, g_r)


def hand_over(*refs):
    count = (len(refs) - 2) // 3
    ins, outs, bufs = refs[:count], refs[count : 2 * count], refs[2 * count : 3 * count]
    in_sem, out_sem = refs[3 * count :]
    moves = []
    for src, dst, buf in zip(ins, outs, bufs):
        n = src.shape[-2] // 2
        for k in range(2):
            cut = (slice(None),) * (len(src.shape) - 2) + (slice(k * n, (k + 1) * n),)
            if n % 16:
                if k:
                    continue
                cut = ()
            i = len(moves)
            part = [r.at[cut] if cut else r for r in (src, buf, dst)]
            moves.append(
                (
                    pltpu.make_async_copy(part[0], part[1], in_sem.at[i]),
                    pltpu.make_async_copy(part[1], part[2], out_sem.at[i]),
                )
            )
    for get, _ in moves:
        get.start()
    for get, put in moves:
        get.wait()
        put.start()
    for _, put in moves:
        put.wait()


def local(
    tokens, cotangent, routes, gates, hot_index, hot_gate, w_gate_up, w_down, w_hot_gu, w_hot_dn
):
    n_dp, n_e = lax.axis_size("dp"), lax.axis_size("expert")
    n_tok, width = tokens.shape
    n_hot = hot_index.shape[0]
    rows_gu, double = w_gate_up.shape[1:]
    rows_dn = w_down.shape[1]
    units, features = w_hot_dn.shape
    n_row = n_e * MSG
    vmem = pl.BlockSpec(memory_space=pltpu.VMEM)
    any_space = pl.BlockSpec(memory_space=pl.ANY)
    msg = (n_e, MSG, 3 * width // 4)
    hot2 = 2 * n_hot
    dma = pltpu.SemaphoreType.DMA
    results = (
        jax.ShapeDtypeStruct((n_tok, width), BF),
        jax.ShapeDtypeStruct((n_tok, width), BF),
        jax.ShapeDtypeStruct(w_gate_up.shape, BF),
        jax.ShapeDtypeStruct(w_down.shape, BF),
        jax.ShapeDtypeStruct((2, features, units), BF),
        jax.ShapeDtypeStruct((features, units), BF),
    )
    outs = pl.pallas_call(
        kernel,
        out_shape=results,
        in_specs=[any_space] * 4 + [vmem] * 6,
        out_specs=(any_space,) * 6,
        scratch_shapes=[
            pltpu.VMEM((n_tok, width), BF),
            pltpu.VMEM((n_tok, width), BF),
            pltpu.VMEM((features, 384), BF),
            pltpu.VMEM((n_tok, width), BF),
            pltpu.VMEM((n_tok, width), BF),
            pltpu.VMEM((3, features, units), BF),
            pltpu.VMEM((n_tok, 1), F32),
            pltpu.VMEM((n_hot, 1), F32),
            pltpu.VMEM((n_dp, rows_gu, double), BF),
            pltpu.VMEM((n_dp, rows_dn, width), BF),
            pltpu.VMEM((n_dp, hot2, width), BF),
            pltpu.VMEM((NZ, NX, features, 384), BF),
            pltpu.VMEM(msg, BF),
            pltpu.VMEM(msg, BF),
            pltpu.VMEM(msg, BF),
            pltpu.VMEM(msg, BF),
            pltpu.VMEM(msg, BF),
            pltpu.VMEM(msg, BF),
            pltpu.VMEM((n_row, width), BF),
            pltpu.VMEM((n_row, width), BF),
            pltpu.VMEM((width, n_row), BF),
            pltpu.VMEM((double // 2, n_row), BF),
            pltpu.VMEM((n_row, double // 2), BF),
            pltpu.VMEM((n_row, double), BF),
            pltpu.VMEM((n_row, double), F32),
            pltpu.VMEM((n_row, double // 2), F32),
            pltpu.VMEM((n_dp, rows_gu, double), BF),
            pltpu.VMEM((n_dp, rows_dn, width), BF),
            pltpu.VMEM((n_dp, hot2, width), BF),
            pltpu.VMEM((NY, rows_gu, double), BF),
            pltpu.VMEM((NY, rows_dn, width), BF),
            pltpu.VMEM((NY, hot2, width), BF),
            pltpu.VMEM((3, rows_gu, double), BF),
            pltpu.VMEM((3, rows_dn, width), BF),
            pltpu.VMEM((3, hot2, width), BF),
            pltpu.VMEM((hot2, width), BF),
            pltpu.VMEM((NZ, NX, features, 384), BF),
            pltpu.VMEM((3, NZ, features, 384), BF),
            pltpu.VMEM((NZ, features, 384), BF),
            dma((112,)),
            dma((112,)),
            dma((n_e,)),
            dma((n_e,)),
            dma((n_e,)),
            dma((n_e,)),
            dma((n_e,)),
            dma((n_e,)),
            dma((n_e,)),
            dma((n_e,)),
            dma((10,)),
        ],
        compiler_params=pltpu.CompilerParams(
            collective_id=0, has_side_effects=True, vmem_limit_bytes=67043328
        ),
        name="expert_layer",
    )(
        tokens, cotangent, w_gate_up, w_down,
        routes.reshape(1, n_tok), gates.reshape(1, n_tok),
        hot_index.reshape(1, n_hot), hot_gate.reshape(1, n_hot),
        w_hot_gu.transpose(0, 2, 1), w_hot_dn.T,
    )
    outs = pl.pallas_call(
        hand_over,
        out_shape=results,
        in_specs=[any_space] * 6,
        out_specs=(any_space,) * 6,
        scratch_shapes=[pltpu.VMEM(r.shape, BF) for r in results] + [dma((12,)), dma((12,))],
        name="hand_over",
    )(*outs)
    layer_out, input_grad, grad_gu, grad_dn, hot_gu, hot_dn = outs
    return layer_out, input_grad, grad_gu, grad_dn, hot_gu.transpose(0, 2, 1), hot_dn.T


def solution(mesh):
    placed = (
        P(("dp", "expert"), None),
        P(("dp", "expert"), None),
        P(("dp", "expert"), None),
        P(("dp", "expert"), None),
        P(("dp", "expert")),
        P(("dp", "expert")),
        P("expert", "dp", None),
        P("expert", "dp", None),
        P(None, "dp", "expert"),
        P("dp", "expert"),
    )
    return jax.shard_map(
        local,
        mesh=mesh,
        in_specs=placed,
        out_specs=(
            P(("dp", "expert"), None),
            P(("dp", "expert"), None),
            P("expert", "dp", None),
            P("expert", "dp", None),
            P(None, "dp", "expert"),
            P("dp", "expert"),
        ),
        check_vma=False,
    )
```

```python
import functools

import jax
import jax.numpy as jnp
from jax import lax
from jax.experimental import pallas as pl
from jax.experimental.pallas import tpu as pltpu
from jax.sharding import PartitionSpec as P

MESH = pl.DeviceIdType.MESH
BF = jnp.bfloat16
F32 = jnp.float32
CAP = 6
MSG = 8
NZ, NX, NY = 8, 4, 4


def dot(a, b):
    return jnp.dot(a, b, preferred_element_type=F32)


def dot_nt(a, b):
    return lax.dot_general(a, b, (((1,), (1,)), ((), ())), preferred_element_type=F32)


def hit(a, b):
    return jnp.where(a == b, 1.0, 0.0).astype(BF)


def iota(shape, axis):
    return lax.broadcasted_iota(jnp.int32, shape, axis)


class Sems:
    def __init__(self, send, recv):
        self.send, self.recv, self.ids = send, recv, {}

    def __call__(self, name):
        if name not in self.ids:
            self.ids[name] = len(self.ids)
        n = self.ids[name]
        return self.send.at[n], self.recv.at[n]


def kernel(
    tok_in, cot_in, wgu_in, wdn_in,
    routes_row, gates_row, hidx_row, hgate_row, hot_gu_in, hot_dn_in,
    lo_out, ig_out, ggu_out, gdn_out, ghg_out, ghd_out,
    tok, cot, hw_in, lo_buf, ig_buf, ghg_buf, gates, hgate,
    wgu, wdn, hxs, hw, send_x, send_s, recv_x, recv_s, back_o, back_g, rx, rs, xt, ht, hid, dact, acc, dh_acc,
    pgu, pdn, phb, qgu, qdn, qhb, rgu, rdn, rhb, hown, hg, hgr, hgz,
    sem_s, sem_r, x_s, x_r, s_s, s_r, o_s, o_r, g_s, g_r, loc,
):
    me, e = lax.axis_index("dp"), lax.axis_index("expert")
    y, c = me // 2, me % 2
    z, x = e // NX, e % NX
    yp, ym, y2 = (y + 1) % NY, (y + 3) % NY, (y + 2) % NY
    xp, xm, x2 = (x + 1) % NX, (x + 3) % NX, (x + 2) % NX
    up, down, mate = (2 * yp + c, e), (2 * ym + c, e), (2 * y + 1 - c, e)
    right, left = (me, NX * z + xp), (me, NX * z + xm)
    sems = Sems(sem_s, sem_r)
    started = []

    def send(name, src, dst, dev):
        s, r = sems(name)
        copy = pltpu.make_async_remote_copy(
            src_ref=src, dst_ref=dst, send_sem=s, recv_sem=r, device_id=dev, device_id_type=MESH
        )
        copy.start()
        started.append(copy)

    def arrived(name, dst):
        s, r = sems(name)
        pltpu.make_async_remote_copy(
            src_ref=dst, dst_ref=dst, send_sem=s, recv_sem=r, device_id=mate, device_id_type=MESH
        ).wait_recv()

    barrier = pltpu.get_barrier_semaphore()
    for dev in (up, down, mate):
        pl.semaphore_signal(barrier, inc=1, device_id=dev, device_id_type=MESH)

    @pl.loop(1, NZ * NX)
    def _(j):
        pl.semaphore_signal(
            barrier, inc=1, device_id=(me, (e + j) % (NZ * NX)), device_id_type=MESH
        )

    def fetch(n, src, dst):
        copy = pltpu.make_async_copy(src, dst, loc.at[n])
        copy.start()
        return copy

    rows_in = (fetch(0, tok_in, tok), fetch(1, cot_in, cot))
    later_in = (
        fetch(2, wgu_in.at[0], wgu.at[me]),
        fetch(3, wdn_in.at[0], wdn.at[me]),
    )

    n_tok, width = tok.shape
    third = 3 * width // 4 // 3
    n_hot = hidx_row.shape[1]

    def turned(row):
        n = row.shape[1]
        return jnp.sum(jnp.where(iota((n, n), 0) == iota((n, n), 1), row, 0.0), axis=1, keepdims=True)

    rr = routes_row[...]
    rc = turned(rr.astype(F32)).astype(jnp.int32)
    gates[...] = turned(gates_row[...])
    hgate[...] = turned(hgate_row[...])
    hidx_col = turned(hidx_row[...].astype(F32)).astype(jnp.int32)
    units = hot_dn_in.shape[1]
    zeros = jnp.zeros((hw_in.shape[0], 128 - units), BF)
    for n, w in enumerate((hot_gu_in[0], hot_gu_in[1], hot_dn_in[...])):
        hw_in[:, n * 128 : (n + 1) * 128] = jnp.concatenate([w, zeros], axis=1)

    for copy in rows_in:
        copy.wait()
    pick_hot = hit(iota((n_hot, n_tok), 1), hidx_col)
    hown[0:n_hot] = dot(pick_hot, tok[...]).astype(BF)
    hown[n_hot:] = (hgate[...] * dot(pick_hot, cot[...])).astype(BF)
    hxs[me] = hown[...]
    hw[z, x] = hw_in[...]

    onehot = hit(iota((NZ * NX, n_tok), 0), rr)
    ahead = jnp.where(iota((n_tok, n_tok), 0) < iota((n_tok, n_tok), 1), 1.0, 0.0).astype(BF)
    pos_r = jnp.sum(dot(onehot, ahead) * onehot.astype(F32), axis=0, keepdims=True).astype(jnp.int32)
    onehot = hit(iota((n_tok, n_tok), 1), rc)
    ahead = jnp.where(iota((n_tok, n_tok), 1) < iota((n_tok, n_tok), 0), 1.0, 0.0).astype(BF)
    pos_c = jnp.sum(dot(ahead, onehot) * onehot.astype(F32), axis=1, keepdims=True).astype(jnp.int32)

    def tail_code(route, pos, i):
        high = jnp.where(pos >= 3, 1, 0)
        return jnp.where(pos - 3 * high == i, route * MSG + CAP + high, -9)

    rows = NZ * NX * MSG
    q_id = iota((rows, n_tok), 0)
    main = hit(q_id, rr * MSG + pos_r)

    def columns(i):
        part = slice(i * third, (i + 1) * third)
        return tok[:, part], (gates[...] * cot[:, part].astype(F32)).astype(BF)

    tails = columns(3)
    for i in range(3):
        choose = jnp.concatenate([main, hit(q_id, tail_code(rr, pos_r, i))], axis=1)
        for out, now, tail in zip((send_x, send_s), columns(i), tails):
            data = dot(choose, jnp.concatenate([now, tail], axis=0))
            out[:, :, i * third : (i + 1) * third] = data.astype(BF).reshape(NZ * NX, MSG, third)
    recv_x[e] = send_x[e]
    recv_s[e] = send_s[e]

    pl.semaphore_wait(barrier, NZ * NX + 2)

    halves = {
        "h": (hown, hxs, hxs.shape[1] // 2),
        "g": (wgu_in.at[0], wgu, wgu.shape[1] // 2),
        "d": (wdn_in.at[0], wdn, wdn.shape[1] // 2),
    }

    def half(name, block, k):
        size = halves[name][2]
        return halves[name][1].at[block, pl.ds(k * size, size)]

    def own_half(name, k):
        size = halves[name][2]
        return halves[name][0].at[pl.ds(k * size, size)]

    def ring_start(names):
        for k in (0, 1):
            for name in names:
                send((name, "up", k), own_half(name, k), half(name, me, k), up)
                send((name, "down", 1 - k), own_half(name, 1 - k), half(name, me, 1 - k), down)
        for name in names:
            send((name, "mate"), halves[name][0], halves[name][1].at[me], mate)

    def ring_near(names, k):
        for name in names:
            low, high = half(name, 2 * ym + c, k), half(name, 2 * yp + c, 1 - k)
            arrived((name, "up", k), low)
            if k == 0:
                send((name, "up", 2), low, low, up)
            send((name, "mate", 0, k), low, low, mate)
            arrived((name, "down", 1 - k), high)
            if k == 0:
                send((name, "down", 2), high, high, down)
            send((name, "mate", 1, k), high, high, mate)

    def ring_far(names):
        for name in names:
            low, high = half(name, 2 * y2 + c, 0), half(name, 2 * y2 + c, 1)
            arrived((name, "up", 2), low)
            send((name, "mate", 2, 0), low, low, mate)
            arrived((name, "down", 2), high)
            send((name, "mate", 2, 1), high, high, mate)

    def ring_end(names, near=True, far=True):
        d = 1 - c
        for name in names:
            if near:
                arrived((name, "mate"), halves[name][1].at[2 * y + d])
            for k in (0, 1):
                if near:
                    arrived((name, "mate", 0, k), half(name, 2 * ym + d, k))
                    arrived((name, "mate", 1, k), half(name, 2 * yp + d, 1 - k))
                if far:
                    arrived((name, "mate", 2, k), half(name, 2 * y2 + d, k))

    ring_start(["h"])
    for j in range(1, NZ):
        send(("hz", j), hw_in, hw.at[z, x], (me, NX * ((z + j) % NZ) + x))

    def token_copy(j, sign, out_ref, in_ref, s, r):
        peer = (e + j) % (NZ * NX) if sign else (e + NZ * NX - j) % (NZ * NX)
        return pltpu.make_async_remote_copy(
            src_ref=out_ref.at[peer] if sign else in_ref.at[peer],
            dst_ref=in_ref.at[e] if sign else in_ref.at[peer],
            send_sem=s.at[j],
            recv_sem=r.at[j],
            device_id=(me, peer),
            device_id_type=MESH,
        )

    def tokens_start(*copy):
        @pl.loop(1, NZ * NX)
        def _(j):
            token_copy(j, True, *copy).start()

    def tokens_wait(*copy):
        @pl.loop(1, NZ * NX)
        def _(j):
            token_copy(j, False, *copy).wait_recv()

    def tokens_sent(*copy):
        @pl.loop(1, NZ * NX)
        def _(j):
            token_copy(j, True, *copy).wait_send()

    ring_start(["d", "g"])
    tokens_start(send_x, recv_x, x_s, x_r)

    ring_near(["h"], 0)
    ring_near(["h"], 1)

    for j in range(1, NZ):
        arrived(("hz", j), hw.at[(z + NZ - j) % NZ, x])

    def hw_half(col, k):
        return hw.at[pl.ds(k * (NZ // 2), NZ // 2), col]

    for k in (0, 1):
        send(("x", "right", k), hw_half(x, k), hw_half(x, k), right)
        send(("x", "left", 1 - k), hw_half(x, 1 - k), hw_half(x, 1 - k), left)
    tokens_start(send_s, recv_s, s_s, s_r)
    ring_far(["h"])
    ring_near(["d", "g"], 0)
    arrived(("x", "right", 0), hw_half(xm, 0))
    send(("x", "right", 2), hw_half(xm, 0), hw_half(xm, 0), right)
    arrived(("x", "left", 1), hw_half(xp, 1))
    send(("x", "left", 2), hw_half(xp, 1), hw_half(xp, 1), left)
    arrived(("x", "right", 1), hw_half(xm, 1))
    arrived(("x", "left", 0), hw_half(xp, 0))
    arrived(("x", "right", 2), hw_half(x2, 0))
    arrived(("x", "left", 2), hw_half(x2, 1))
    ring_end(["h"])
    for copy in later_in:
        copy.wait()

    n_dp = hxs.shape[0]
    n_all = n_dp * n_hot
    hot_x = hxs[:, 0:n_hot, :].reshape(n_all, width)
    hot_s = hxs[:, n_hot:, :].reshape(n_all, width)
    act = dot(hot_x, hw[:, :, :, 0:256].reshape(width, 256))
    hot_g, hot_u = act[:, 0:128], act[:, 128:256]
    hot_dh = dot(hot_s, hw[:, :, :, 256:384].reshape(width, 128))
    sigma = 1.0 / (1.0 + jnp.exp(-hot_g))
    hot_h = (hot_g * sigma * hot_u).astype(BF)
    hot_d = jnp.concatenate(
        [
            (hot_dh * hot_u * sigma * (1.0 + hot_g * (1.0 - sigma))).astype(BF),
            (hot_dh * hot_g * sigma).astype(BF),
        ],
        axis=1,
    )
    quarter = width // 4
    for k in range(4):
        part = slice(k * quarter, (k + 1) * quarter)
        zs = slice(2 * k, 2 * k + 2)
        w_gu = hw[zs, :, :, 0:256].reshape(quarter, 256)
        w_dn = hw[zs, :, :, 256:384].reshape(quarter, 128)
        phb[:, 0:n_hot, part] = dot_nt(hot_h, w_dn).astype(BF).reshape(n_dp, n_hot, quarter)
        phb[:, n_hot:, part] = dot_nt(hot_d, w_gu).astype(BF).reshape(n_dp, n_hot, quarter)
        x_t = hxs[:, 0:n_hot, part].reshape(n_all, quarter).T
        s_t = hxs[:, n_hot:, part].reshape(n_all, quarter).T
        block = (2, NX, hw.shape[2])
        hg[zs, :, :, 0:256] = dot(x_t, hot_d).astype(BF).reshape(*block, 256)
        hg[zs, :, :, 256:384] = dot(s_t, hot_h).astype(BF).reshape(*block, 128)

    sums = {
        "h": (phb, qhb, rhb, hxs.shape[1] // 2, 32),
        "g": (pgu, qgu, rgu, wgu.shape[1] // 2, 32),
        "d": (pdn, qdn, rdn, wdn.shape[1] // 2, 48),
    }

    def chip_send(name, yy):
        p, q = sums[name][0:2]
        send((name, "chip", (yy,)), p.at[2 * CHIP[yy] + 1 - c], q.at[CHIP[yy]], mate)

    CHIP = {"y": y, "p": yp, "m": ym, "2": y2}

    def chip_add(name, yy):
        p, q, _, size, step = sums[name]
        arrived((name, "chip", (yy,)), q.at[CHIP[yy]])

        @pl.loop(0, 2 * size // step)
        def _(i):
            part = pl.ds(pl.multiple_of(i * step, step), step)
            q[CHIP[yy], part] = (
                q[CHIP[yy], part].astype(F32) + p[2 * CHIP[yy] + c, part].astype(F32)
            ).astype(BF)

    def q_half(name, yy, k):
        size = sums[name][3]
        return sums[name][1].at[CHIP[yy], pl.ds(k * size, size)]

    def r_half(name, slot, k):
        size = sums[name][3]
        return sums[name][2].at[slot, pl.ds(k * size, size)]

    def far_send(name):
        send((name, "far", 0), q_half(name, "2", 0), r_half(name, 0, 0), up)
        send((name, "far", 1), q_half(name, "2", 1), r_half(name, 0, 1), down)

    def near_send(name, first):
        if first:
            send((name, "sum", 0), q_half(name, "p", 1), r_half(name, 1, 1), up)
            send((name, "sum", 1), q_half(name, "m", 0), r_half(name, 2, 0), down)
        else:
            send((name, "sum", 2), q_half(name, "p", 0), r_half(name, 1, 0), up)
            send((name, "sum", 3), q_half(name, "m", 1), r_half(name, 2, 1), down)

    def near_add(name):
        _, q, r, size, step = sums[name]
        step = min(step, size)
        for k, yy in ((0, "p"), (1, "m")):
            arrived((name, "far", k), r_half(name, 0, k))

            @pl.loop(0, size // step)
            def _(i):
                part = pl.ds(pl.multiple_of(k * size + i * step, 16), step)
                q[CHIP[yy], part] = (
                    q[CHIP[yy], part].astype(F32) + r[0, part].astype(F32)
                ).astype(BF)

    def sum_wait(name):
        arrived((name, "sum", 0), r_half(name, 1, 1))
        arrived((name, "sum", 1), r_half(name, 2, 0))
        arrived((name, "sum", 2), r_half(name, 1, 0))
        arrived((name, "sum", 3), r_half(name, 2, 1))

    for yy in "2pmy":
        chip_send("h", yy)

    def hg_half(col, k):
        return hg.at[pl.ds(k * (NZ // 2), NZ // 2), col]

    def hgr_half(slot, k):
        return hgr.at[slot, pl.ds(k * (NZ // 2), NZ // 2)]

    send(("gx", "far", 0), hg_half(x2, 0), hgr_half(0, 0), right)
    send(("gx", "far", 1), hg_half(x2, 1), hgr_half(0, 1), left)
    send(("gx", "sum", 0), hg_half(xp, 1), hgr_half(1, 1), right)
    send(("gx", "sum", 1), hg_half(xm, 0), hgr_half(2, 0), left)

    ring_near(["d", "g"], 1)
    for yy in "2pmy":
        chip_add("h", yy)
    far_send("h")
    near_send("h", True)

    n_row = rows
    hidden = wdn.shape[0] * wdn.shape[1]
    w_dn2 = wdn.reshape(hidden, width)
    chip_rows = 2 * wgu.shape[1]
    row_id, col_id = iota((rows, rows), 0), iota((rows, rows), 1)
    kept = (iota((rows, 1), 0) & (MSG - 1)) < CAP

    def spread_tail(a, b, i):
        place = a & (MSG - 1)
        return hit(b, jnp.where(place < CAP, tail_code(a >> 3, place, i), -9))

    def rows_of(message, out):
        tail = None
        for i in range(3):
            part = slice(i * third, (i + 1) * third)
            data = message[:, :, part].reshape(rows, third)
            out[:, part] = jnp.where(kept, data, jnp.zeros_like(data))
            piece = dot(spread_tail(row_id, col_id, i), data)
            tail = piece if tail is None else tail + piece
        out[:, 3 * third :] = tail.astype(BF)

    def message_of(data, out):
        for i in range(3):
            part = slice(i * third, (i + 1) * third)
            moved = dot(spread_tail(col_id, row_id, i), data[:, 3 * third :])
            out[:, :, part] = (
                jnp.where(kept, data[:, part].astype(F32), moved).astype(BF).reshape(NZ * NX, MSG, third)
            )

    def act_block(yy, part):
        ks = pl.ds(pl.multiple_of(CHIP[yy] * chip_rows, 128), chip_rows)
        w = wgu[pl.ds(2 * CHIP[yy], 2), :, part].reshape(chip_rows, 256)
        return dot(rx[:, ks], w)

    tokens_wait(send_x, recv_x, x_s, x_r)
    rows_of(recv_x, rx)
    for k in range(4):
        part = slice(k * third, (k + 1) * third)
        xt[part] = rx[:, part].T
    ring_end(["d", "g"], far=False)

    @pl.loop(0, 2 * hidden // 256)
    def _(n):
        part = pl.ds(pl.multiple_of(n * 256, 256), 256)
        acc[:, part] = act_block("y", part) + act_block("m", part) + act_block("p", part)

    arrived(("gx", "far", 0), hgr_half(0, 0))
    arrived(("gx", "far", 1), hgr_half(0, 1))
    for k, col in ((0, xp), (1, xm)):
        for i in range(NZ // 2):
            n = k * (NZ // 2) + i
            hg[n, col] = (hg[n, col].astype(F32) + hgr[0, n].astype(F32)).astype(BF)
    send(("gx", "sum", 2), hg_half(xp, 0), hgr_half(1, 0), right)
    send(("gx", "sum", 3), hg_half(xm, 1), hgr_half(2, 1), left)

    ring_far(["d"])
    tokens_wait(send_s, recv_s, s_s, s_r)
    rows_of(recv_s, rs)
    ring_far(["g"])
    ring_end(["d"], near=False)

    @pl.loop(0, hidden // 256)
    def _(n):
        part = pl.ds(pl.multiple_of(n * 256, 256), 256)
        dh_acc[:, part] = dot_nt(rs[...], w_dn2[part])

    near_add("h")
    near_send("h", False)
    ring_end(["g"], near=False)

    @pl.loop(0, hidden // 256)
    def _(n):
        first = pl.ds(pl.multiple_of(n * 256, 256), 256)
        second = pl.ds(pl.multiple_of(hidden + n * 256, 256), 256)
        g = acc[:, first] + act_block("2", first)
        u = acc[:, second] + act_block("2", second)
        dh = dh_acc[:, first]
        s = 1.0 / (1.0 + jnp.exp(-g))
        h = (g * s * u).astype(BF)
        hid[:, first] = h
        ht[first] = h.T
        dact[:, first] = (dh * u * s * (1.0 + g * (1.0 - s))).astype(BF)
        dact[:, second] = (dh * g * s).astype(BF)

    half_rows = wgu.shape[1]

    def grad_gu(yy):
        lhs = xt[pl.ds(pl.multiple_of(CHIP[yy] * 2 * half_rows, 16), 2 * half_rows)]

        @pl.loop(0, 2 * hidden // 256)
        def _(n):
            part = pl.ds(pl.multiple_of(n * 256, 256), 256)
            both = dot(lhs, dact[:, part]).astype(BF)
            pgu[pl.ds(2 * CHIP[yy], 2), :, part] = both.reshape(2, half_rows, 256)

        chip_send("g", yy)

    grad_gu("2")
    arrived(("gx", "sum", 0), hgr_half(1, 1))
    arrived(("gx", "sum", 1), hgr_half(2, 0))
    arrived(("gx", "sum", 2), hgr_half(1, 0))
    arrived(("gx", "sum", 3), hgr_half(2, 1))
    for n in range(NZ):
        hg[n, x] = (
            hg[n, x].astype(F32) + hgr[1, n].astype(F32) + hgr[2, n].astype(F32)
        ).astype(BF)
    hgz[z] = hg[z, x]
    for j in range(1, NZ):
        there = (z + j) % NZ
        send(("gz", j), hg.at[there, x], hgz.at[z], (me, NX * there + x))

    @pl.loop(0, width // 256)
    def _(n):
        part = pl.ds(pl.multiple_of(n * 256, 256), 256)
        rx[:, part] = dot(hid[...], w_dn2[:, part]).astype(BF)

    chip_add("g", "2")
    far_send("g")

    tokens_sent(send_x, recv_x, x_s, x_r)
    message_of(rx, send_x)
    back_o[e] = send_x[e]
    tokens_start(send_x, back_o, o_s, o_r)

    @pl.loop(0, width // 256)
    def _(n):
        part = pl.ds(pl.multiple_of(n * 256, 256), 256)
        pdn[:, :, part] = dot(ht[...], rs[:, part]).astype(BF).reshape(*pdn.shape[0:2], 256)

    for yy in "2pmy":
        chip_send("d", yy)
    grad_gu("p")
    chip_add("d", "2")
    far_send("d")
    grad_gu("m")
    for k in range(wgu.shape[0] // 2):
        w = wgu[2 * k : 2 * k + 2].reshape(chip_rows, 2 * hidden)
        rs[:, k * chip_rows : (k + 1) * chip_rows] = dot_nt(dact[...], w).astype(BF)
    tokens_sent(send_s, recv_s, s_s, s_r)
    message_of(rs, send_s)
    back_g[e] = send_s[e]
    tokens_start(send_s, back_g, g_s, g_r)
    for yy in "pm":
        for name in "gd":
            chip_add(name, yy)
    for name in "gd":
        near_send(name, True)
    for name in "gd":
        near_add(name)
        near_send(name, False)
    grad_gu("y")
    for name in "gd":
        chip_add(name, "y")

    leaving = []
    sum_wait("h")
    hot_sum = qhb[y].astype(F32) + rhb[1].astype(F32) + rhb[2].astype(F32)
    back = jnp.concatenate([hgate[...] * hot_sum[0:n_hot], hot_sum[n_hot:]], axis=1)
    upper = back.astype(BF)
    lower = (back - upper.astype(F32)).astype(BF)
    spread = hit(iota((n_tok, n_hot), 0), hidx_row[...])

    lane_id = iota((n_tok, rows), 1)
    straight = hit(lane_id, rc * MSG + pos_c)
    bent = [hit(lane_id, tail_code(rc, pos_c, i)) for i in range(3)]

    def results(back_ref, hot_first, out):
        tail = None
        for i in range(4):
            part = slice(i * third, (i + 1) * third)
            if i < 3:
                data = back_ref[:, :, part].reshape(rows, third)
                got = dot(straight, data)
                piece = dot(bent[i], data)
                tail = piece if tail is None else tail + piece
            else:
                got = tail
            lanes = slice(hot_first + i * third, hot_first + (i + 1) * third)
            hot_part = dot(spread, upper[:, lanes]) + dot(spread, lower[:, lanes])
            if hot_first == 0:
                got = gates[...] * got
            out[:, part] = (got + hot_part).astype(BF)

    tokens_wait(send_x, back_o, o_s, o_r)
    results(back_o, 0, lo_buf)
    leaving.append(fetch(6, lo_buf, lo_out))
    tokens_wait(send_s, back_g, g_s, g_r)
    results(back_g, width, ig_buf)
    leaving.append(fetch(7, ig_buf, ig_out))
    scale = 1.0 / 32.0
    total = hgz[z].astype(F32)
    for j in range(1, NZ):
        there = (z + NZ - j) % NZ
        arrived(("gz", j), hgz.at[there])
        total = total + hgz[there].astype(F32)
    total = (total * scale).astype(BF)
    ghg_buf[0] = total[:, 0:units]
    ghg_buf[1] = total[:, 128 : 128 + units]
    ghg_buf[2] = total[:, 256 : 256 + units]
    leaving.append(fetch(8, ghg_buf.at[0:2], ghg_out))
    leaving.append(fetch(9, ghg_buf.at[2], ghd_out))


    for n, (name, out) in enumerate((("g", ggu_out), ("d", gdn_out))):
        _, q, r, size, step = sums[name]
        sum_wait(name)

        @pl.loop(0, 2 * size // step)
        def _(i):
            part = pl.ds(pl.multiple_of(i * step, step), step)
            value = q[y, part].astype(F32) + r[1, part].astype(F32) + r[2, part].astype(F32)
            q[y, part] = (value * scale).astype(BF)

        leaving.append(fetch(n, q.at[y], out.at[0]))

    for copy in started:
        copy.wait_send()
    for copy in leaving:
        copy.wait()

    tokens_sent(send_x, back_o, o_s, o_r)
    tokens_sent(send_s, back_g, g_s, g_r)


def hand_over(*refs):
    count = (len(refs) - 2) // 3
    ins, outs, bufs = refs[:count], refs[count : 2 * count], refs[2 * count : 3 * count]
    in_sem, out_sem = refs[3 * count :]
    moves = []
    for src, dst, buf in zip(ins, outs, bufs):
        n = src.shape[-2] // 2
        for k in range(2):
            cut = (slice(None),) * (len(src.shape) - 2) + (slice(k * n, (k + 1) * n),)
            if n % 16:
                if k:
                    continue
                cut = ()
            i = len(moves)
            part = [r.at[cut] if cut else r for r in (src, buf, dst)]
            moves.append(
                (
                    pltpu.make_async_copy(part[0], part[1], in_sem.at[i]),
                    pltpu.make_async_copy(part[1], part[2], out_sem.at[i]),
                )
            )
    for get, _ in moves:
        get.start()
    for get, put in moves:
        get.wait()
        put.start()
    for _, put in moves:
        put.wait()


def local(
    tokens, cotangent, routes, gates, hot_index, hot_gate, w_gate_up, w_down, w_hot_gu, w_hot_dn
):
    n_dp, n_e = lax.axis_size("dp"), lax.axis_size("expert")
    n_tok, width = tokens.shape
    n_hot = hot_index.shape[0]
    rows_gu, double = w_gate_up.shape[1:]
    rows_dn = w_down.shape[1]
    units, features = w_hot_dn.shape
    n_row = n_e * MSG
    vmem = pl.BlockSpec(memory_space=pltpu.VMEM)
    any_space = pl.BlockSpec(memory_space=pl.ANY)
    msg = (n_e, MSG, 3 * width // 4)
    hot2 = 2 * n_hot
    dma = pltpu.SemaphoreType.DMA
    results = (
        jax.ShapeDtypeStruct((n_tok, width), BF),
        jax.ShapeDtypeStruct((n_tok, width), BF),
        jax.ShapeDtypeStruct(w_gate_up.shape, BF),
        jax.ShapeDtypeStruct(w_down.shape, BF),
        jax.ShapeDtypeStruct((2, features, units), BF),
        jax.ShapeDtypeStruct((features, units), BF),
    )
    outs = pl.pallas_call(
        kernel,
        out_shape=results,
        in_specs=[any_space] * 4 + [vmem] * 6,
        out_specs=(any_space,) * 6,
        scratch_shapes=[
            pltpu.VMEM((n_tok, width), BF),
            pltpu.VMEM((n_tok, width), BF),
            pltpu.VMEM((features, 384), BF),
            pltpu.VMEM((n_tok, width), BF),
            pltpu.VMEM((n_tok, width), BF),
            pltpu.VMEM((3, features, units), BF),
            pltpu.VMEM((n_tok, 1), F32),
            pltpu.VMEM((n_hot, 1), F32),
            pltpu.VMEM((n_dp, rows_gu, double), BF),
            pltpu.VMEM((n_dp, rows_dn, width), BF),
            pltpu.VMEM((n_dp, hot2, width), BF),
            pltpu.VMEM((NZ, NX, features, 384), BF),
            pltpu.VMEM(msg, BF),
            pltpu.VMEM(msg, BF),
            pltpu.VMEM(msg, BF),
            pltpu.VMEM(msg, BF),
            pltpu.VMEM(msg, BF),
            pltpu.VMEM(msg, BF),
            pltpu.VMEM((n_row, width), BF),
            pltpu.VMEM((n_row, width), BF),
            pltpu.VMEM((width, n_row), BF),
            pltpu.VMEM((double // 2, n_row), BF),
            pltpu.VMEM((n_row, double // 2), BF),
            pltpu.VMEM((n_row, double), BF),
            pltpu.VMEM((n_row, double), F32),
            pltpu.VMEM((n_row, double // 2), F32),
            pltpu.VMEM((n_dp, rows_gu, double), BF),
            pltpu.VMEM((n_dp, rows_dn, width), BF),
            pltpu.VMEM((n_dp, hot2, width), BF),
            pltpu.VMEM((NY, rows_gu, double), BF),
            pltpu.VMEM((NY, rows_dn, width), BF),
            pltpu.VMEM((NY, hot2, width), BF),
            pltpu.VMEM((3, rows_gu, double), BF),
            pltpu.VMEM((3, rows_dn, width), BF),
            pltpu.VMEM((3, hot2, width), BF),
            pltpu.VMEM((hot2, width), BF),
            pltpu.VMEM((NZ, NX, features, 384), BF),
            pltpu.VMEM((3, NZ, features, 384), BF),
            pltpu.VMEM((NZ, features, 384), BF),
            dma((112,)),
            dma((112,)),
            dma((n_e,)),
            dma((n_e,)),
            dma((n_e,)),
            dma((n_e,)),
            dma((n_e,)),
            dma((n_e,)),
            dma((n_e,)),
            dma((n_e,)),
            dma((10,)),
        ],
        compiler_params=pltpu.CompilerParams(
            collective_id=0, has_side_effects=True, vmem_limit_bytes=67043328
        ),
        name="expert_layer",
    )(
        tokens, cotangent, w_gate_up, w_down,
        routes.reshape(1, n_tok), gates.reshape(1, n_tok),
        hot_index.reshape(1, n_hot), hot_gate.reshape(1, n_hot),
        w_hot_gu.transpose(0, 2, 1), w_hot_dn.T,
    )
    outs = pl.pallas_call(
        hand_over,
        out_shape=results,
        in_specs=[any_space] * 6,
        out_specs=(any_space,) * 6,
        scratch_shapes=[pltpu.VMEM(r.shape, BF) for r in results] + [dma((12,)), dma((12,))],
        name="hand_over",
    )(*outs)
    layer_out, input_grad, grad_gu, grad_dn, hot_gu, hot_dn = outs
    return layer_out, input_grad, grad_gu, grad_dn, hot_gu.transpose(0, 2, 1), hot_dn.T


def solution(mesh):
    placed = (
        P(("dp", "expert"), None),
        P(("dp", "expert"), None),
        P(("dp", "expert"), None),
        P(("dp", "expert"), None),
        P(("dp", "expert")),
        P(("dp", "expert")),
        P("expert", "dp", None),
        P("expert", "dp", None),
        P(None, "dp", "expert"),
        P("dp", "expert"),
    )
    return jax.shard_map(
        local,
        mesh=mesh,
        in_specs=placed,
        out_specs=(
            P(("dp", "expert"), None),
            P(("dp", "expert"), None),
            P("expert", "dp", None),
            P("expert", "dp", None),
            P(None, "dp", "expert"),
            P("dp", "expert"),
        ),
        check_vma=False,
    )
```
